32 devices in a mesh: grp: 2 (over core), ctx: 8 (over z, x), hd: 2 (over y).
Axes of the slice: x: 2, y: 2, z: 4, core: 2. Of those that a mesh axis runs over, the one named last changes fastest.
Arguments:
- video_q: bfloat16 [1024, 24, 128], P(('ctx', 'hd'), 'grp'), may hold values from -6 to 6
- video_k: bfloat16 [1024, 24, 128], P(('ctx', 'hd'), 'grp'), may hold values from -6 to 6
- video_v: bfloat16 [1024, 24, 128], P(('ctx', 'hd'), 'grp'), may hold values from -6 to 6
- positions: int32 [3, 1024], P(None, ('ctx', 'hd')), may hold values from 0 to 15, as said below
- text_q: bfloat16 [256, 24, 128], P(None, ('grp', 'hd')), may hold values from -16 to 16
- text_k: bfloat16 [256, 24, 128], P(None, ('grp', 'hd')), may hold values from -16 to 16
- text_v: bfloat16 [256, 24, 128], P(None, ('grp', 'hd')), may hold values from -6 to 6
- text_count: int32 [1], replicated, may hold values from 64 to 256
Outputs:
- video_out: bfloat16 [1024, 24, 128], P(('ctx', 'hd'), 'grp')
- text_out: bfloat16 [256, 24, 128], P('ctx', ('grp', 'hd'))
The draws below stay inside these ranges and needn't reach their ends.
Inputs may be any that keep to these rules, and one draw needn't show every extreme that they name: `positions`: column n holds the frame, row and column of video token n; the columns are distinct cells of a grid of 4 frames of 16 by 16 cells.
All inputs are finite; a program needn't handle non-finite values.
Results may differ from the reference program's by a relative error of at most 0.0073.
Values may be sent and summed in bfloat16 or wider, within the bound.
A program may use at most 128 MiB of HBM per device.

```python
import math
import jax
import jax.numpy as jnp
from jax import lax

HEADS = 24
HD = 128
TXT = 256
GRID_H = 16
GRID_W = 16
TOKENS = 1024


def text_pair(key):
    array_shape = (TXT, HEADS, HD)
    keys_base = jnp.clip(jax.random.normal(jax.random.fold_in(key, 101), array_shape, jnp.float32), -3.2, 3.2)
    query_base = jnp.clip(jax.random.normal(jax.random.fold_in(key, 102), array_shape, jnp.float32), -3.2, 3.2)
    return (query_base, keys_base)


def draw_text_q(key, part):
    return text_pair(key)[0].astype(jnp.bfloat16)


def draw_text_k(key, part):
    return text_pair(key)[1].astype(jnp.bfloat16)


def draw_positions(key, part):
    ordering = jax.random.permutation(jax.random.fold_in(key, 7), TOKENS)
    cell_count = GRID_H * GRID_W
    frame_at = ordering // cell_count
    row_at = ordering // GRID_W % GRID_H
    column = ordering % GRID_W
    return jnp.stack([frame_at, row_at, column]).astype(jnp.int32)


def steps_of(stream_key, extent, shards, least, high):
    level = 1.0
    for axis_at, shards_of in shards:
        heights = jax.random.uniform(jax.random.fold_in(jax.random.fold_in(stream_key, 6), axis_at), (shards_of,), jnp.float32, least / len(shards), high / len(shards))
        level = level * jnp.repeat(jnp.exp(heights), extent[axis_at] // shards_of).reshape((-1,) + (1,) * (len(extent) - 1 - axis_at))
    return level


def gaussian(own_key, extent, deviation, bound, cuts=(), held_as=jnp.bfloat16):
    loudness = steps_of(own_key, extent, cuts, -0.22, 0.18) if cuts else 1.0
    entries = jax.random.normal(own_key, extent, jnp.float32) * deviation * loudness
    return jnp.minimum(jnp.maximum(entries, -bound), bound).astype(held_as)


def setup_inputs(seed: int = 0) -> dict:
    arg_keys = jax.random.split(jax.random.key(seed), 9)
    return {
        "video_q": gaussian(arg_keys[0], (TOKENS, HEADS, HD), 1.0, 6.0, ((0, 16), (1, 2))),
        "video_k": gaussian(arg_keys[1], (TOKENS, HEADS, HD), 1.0, 6.0, ((0, 16), (1, 2))),
        "video_v": gaussian(arg_keys[2], (TOKENS, HEADS, HD), 1.0, 6.0, ((0, 16), (1, 2))),
        "positions": draw_positions(jax.random.fold_in(arg_keys[8], 71), 0),
        "text_q": draw_text_q(jax.random.fold_in(arg_keys[8], 71), 0),
        "text_k": draw_text_k(jax.random.fold_in(arg_keys[8], 71), 0),
        "text_v": gaussian(arg_keys[6], (TXT, HEADS, HD), 1.0, 6.0, ((1, 4),)),
        "text_count": jax.random.randint(arg_keys[7], (1,), TXT // 4, TXT + 1).astype(jnp.int32),
    }


THETA = 256.0

def rotate(tokens_in, positions):
    head_dim = tokens_in.shape[-1]
    band_t = head_dim // 8
    band_h = (head_dim - band_t) // 2
    band_w = head_dim - band_t - band_h
    values = tokens_in.astype(jnp.float32)
    pieces = []
    offset = 0
    for axis_index, band_size in ((0, band_t), (1, band_h), (2, band_w)):
        half_size = band_size // 2
        frequency = THETA ** (-2.0 * jnp.arange(half_size, dtype=jnp.float32) / band_size)
        angles = positions[axis_index].astype(jnp.float32)[:, None] * frequency[None, :]
        cos_table = jnp.cos(angles)[:, None, :]
        sin_table = jnp.sin(angles)[:, None, :]
        lower_half = values[:, :, offset:offset + half_size]
        upper_half = values[:, :, offset + half_size:offset + band_size]
        pieces.append(lower_half * cos_table - upper_half * sin_table)
        pieces.append(upper_half * cos_table + lower_half * sin_table)
        offset += band_size
    return jnp.concatenate(pieces, axis=-1).astype(jnp.bfloat16)

def reference(video_q, video_k, video_v, positions, text_q, text_k, text_v, text_count):
    rot_q = rotate(video_q, positions)
    rot_k = rotate(video_k, positions)
    queries = jnp.moveaxis(jnp.concatenate([rot_q, text_q], axis=0), 1, 0)
    keys_all = jnp.moveaxis(jnp.concatenate([rot_k, text_k], axis=0), 1, 0)
    values_all = jnp.moveaxis(jnp.concatenate([video_v, text_v], axis=0), 1, 0)
    live = jnp.concatenate([jnp.ones((TOKENS,), dtype=bool), jnp.arange(TXT, dtype=jnp.int32) < text_count[0]])
    scale = 1.0 / math.sqrt(HD)

    def head_attention(operands):
        q_head, k_head, v_head = operands
        scores = jnp.dot(q_head, k_head.T, preferred_element_type=jnp.float32) * scale
        scores = jnp.where(live[None, :], scores, -jnp.inf)
        peak = lax.optimization_barrier(jnp.max(scores, axis=1, keepdims=True))
        probs = jnp.exp(scores - peak)
        total = lax.optimization_barrier(jnp.sum(probs, axis=1, keepdims=True))
        mixed = jnp.dot(probs.astype(jnp.bfloat16), v_head, preferred_element_type=jnp.float32)
        return (mixed / total).astype(jnp.bfloat16)
    attended = jnp.moveaxis(lax.map(head_attention, (queries, keys_all, values_all)), 0, 1)
    video_out = attended[:TOKENS]
    text_out = attended[TOKENS:]
    return (video_out, text_out)
```

```python
import functools
import math

import jax
import jax.numpy as jnp
import numpy as np
from jax import lax
from jax.experimental import pallas as pl
from jax.experimental.pallas import tpu as pltpu
from jax.sharding import PartitionSpec as P

THETA = 256.0
MESH = pl.DeviceIdType.MESH
PAIR = 2
NEAR = 2


def bands(dim):
    band_t = dim // 8
    band_h = (dim - band_t) // 2
    return (band_t, band_h, dim - band_t - band_h)


def constants(dim):
    freq = np.zeros((dim,), np.float32)
    swap = np.zeros((dim, dim), np.float32)
    start = 0
    for size in bands(dim):
        half = size // 2
        for i in range(half):
            low, high = start + i, start + half + i
            freq[low] = freq[high] = np.float32(THETA ** (-2.0 * i / size))
            swap[high, low] = -1.0
            swap[low, high] = 1.0
        start += size
    return freq, swap


def each(count, body):
    if count <= 4:
        for i in range(count):
            body(i)
    else:
        lax.fori_loop(0, count, lambda i, _: (body(i), 0)[1], 0)


def kernel(far, hds, q_ref, k_ref, v_ref, tq_ref, tk_ref, tv_ref, pos_in, freq_in, swap_in, count_ref,
           out_ref, tout_ref, pos_ref, freq_ref, swap_ref, qin, kin, tqs, tks, tvs, qs, ks, qg, kv, ost, tst, acc, peak, total, probs,
           in_sems, a_send, q_recv, kv_recv, f_send, n_send, o_send, o_recv, t_sems):
    ctx = lax.axis_index("ctx")
    hd = lax.axis_index("hd")
    fi, mi, ni = ctx // (PAIR * NEAR), (ctx // NEAR) % PAIR, ctx % NEAR
    groups = PAIR * hds
    heads = v_ref.shape[1]
    tokens, dim = v_ref.shape[2], v_ref.shape[3]
    mine = hd * PAIR + mi
    slot = fi * NEAR + ni

    def at(f, m, n, h):
        return {"ctx": (f * PAIR + m) * NEAR + n, "hd": h}

    def group_of(d):
        return lax.rem(hd + d // PAIR, hds) * PAIR + lax.rem(mi + d % PAIR, PAIR)

    def group_peer(d):
        g = group_of(d)
        return g, at(fi, g % PAIR, ni, g // PAIR)

    straight_first = [d for d in range(PAIR, groups, PAIR)]
    rest = [d for d in range(1, groups) if d % PAIR]
    early = [(0, 0), (1, 0)] + [(w, d) for d in straight_first for w in range(2)] + [(0, d) for d in rest]
    late = [(1, d) for d in rest]

    def far_peer(d):
        f = lax.rem(fi + d, far)
        return f, at(f, mi, ni, hd)

    def near_peer(d):
        n = lax.rem(ni + d, NEAR)
        return n, at(fi, mi, n, hd)

    text_heads = pl.ds(mi * heads, heads)
    k_in = pltpu.make_async_copy(k_ref, kin, in_sems.at[0])
    q_in = pltpu.make_async_copy(q_ref, qin, in_sems.at[1])
    v_in = pltpu.make_async_copy(v_ref.at[mine], kv.at[slot, 1, mine], in_sems.at[2])
    text_in = (
        pltpu.make_async_copy(tq_ref.at[text_heads], tqs, in_sems.at[3]),
        pltpu.make_async_copy(tk_ref.at[text_heads], tks, in_sems.at[4]),
        pltpu.make_async_copy(tv_ref.at[text_heads], tvs, in_sems.at[5]),
    )
    table_in = (
        pltpu.make_async_copy(pos_in, pos_ref, in_sems.at[6]),
        pltpu.make_async_copy(freq_in, freq_ref, in_sems.at[7]),
        pltpu.make_async_copy(swap_in, swap_ref, in_sems.at[8]),
    )
    barrier = pltpu.get_barrier_semaphore()

    def greet(peer):
        pl.semaphore_signal(barrier, inc=1, device_id=peer, device_id_type=MESH)

    each(groups - 1, lambda i: greet(group_peer(i + 1)[1]))
    each(far - 1, lambda i: greet(far_peer(i + 1)[1]))
    each(NEAR - 1, lambda i: greet(near_peer(i + 1)[1]))

    for copy in table_in + (k_in, q_in, v_in) + text_in:
        copy.start()
    for copy in table_in:
        copy.wait()
    swap = swap_ref[...]
    diagonal = (lax.broadcasted_iota(jnp.int32, (tokens, tokens), 0)
                == lax.broadcasted_iota(jnp.int32, (tokens, tokens), 1))
    lane = lax.broadcasted_iota(jnp.int32, (tokens, dim), 1)

    def column(axis):
        row = pos_ref[axis:axis + 1, :].astype(jnp.float32)
        return jnp.sum(jnp.where(diagonal, row, 0.0), axis=1, keepdims=True)

    band_t, band_h, _ = bands(dim)
    angle = jnp.where(lane < band_t, column(0), jnp.where(lane < band_t + band_h, column(1), column(2))) * freq_ref[...]
    cos, sin = jnp.cos(angle), jnp.sin(angle)

    def rotate(src, dst):
        for g in range(groups):
            for h in range(heads):
                x = src[g, h]
                turned = jnp.dot(x, swap, preferred_element_type=jnp.float32)
                dst[g, h] = (x.astype(jnp.float32) * cos + turned * sin).astype(jnp.bfloat16)

    k_in.wait()
    rotate(kin, ks)
    q_in.wait()
    rotate(qin, qs)
    kv[slot, 0, mine] = ks[mine]
    qg[mine] = qs[mine]
    v_in.wait()
    pl.semaphore_wait(barrier, (groups - 1) + (far - 1) + (NEAR - 1))

    def remote(src, dst, send, recv, peer):
        return pltpu.make_async_remote_copy(src_ref=src, dst_ref=dst, send_sem=send, recv_sem=recv,
                                            device_id=peer, device_id_type=MESH)

    def kv_to_group(w, d):
        g, peer = group_peer(d)
        src = ks if w == 0 else v_ref
        return remote(src.at[g], kv.at[slot, w, mine], a_send.at[w, d], kv_recv.at[slot, w, mine], peer)

    def q_to_group(d):
        g, peer = group_peer(d)
        return remote(qs.at[g], qg.at[mine], a_send.at[2, d], q_recv.at[mine], peer)

    def kv_to_far(w, g, d):
        f, peer = far_peer(d)
        piece = kv.at[slot, w, g]
        return remote(piece, piece, f_send.at[d, w, g], kv_recv.at[slot, w, g], peer)

    def kv_to_near(s, w, g, d):
        n, peer = near_peer(d)
        piece = kv.at[s, w, g]
        return remote(piece, piece, n_send.at[s // NEAR, w, g], kv_recv.at[s, w, g], peer)

    def arrived(s, w, g):
        piece = kv.at[s, w, g]
        remote(piece, piece, n_send.at[0, w, g], kv_recv.at[s, w, g], near_peer(1)[1]).wait_recv()

    def spread(w, g):
        each(far - 1, lambda i: kv_to_far(w, g, i + 1).start())
        kv_to_near(slot, w, g, 1).start()

    for w, d in (early + late)[2:]:
        kv_to_group(w, d).start()
    for d in straight_first + rest:
        q_to_group(d).start()
    for w in range(2):
        spread(w, mine)
    for w, d in (early + late)[2:]:
        g = group_of(d)
        arrived(slot, w, g)
        spread(w, g)

    scale = math.log2(math.e) / math.sqrt(dim)
    rows = groups * tokens

    def queries(h):
        own_text = [tqs[h, (fi * PAIR + m) * NEAR + ni] for m in range(PAIR)]
        return jnp.concatenate([qg[:, h].reshape(rows, dim)] + own_text, axis=0)

    def score(h, keys):
        return lax.dot_general(queries(h), keys, (((1,), (1,)), ((), ())), preferred_element_type=jnp.float32) * scale

    for d in range(1, groups):
        g = group_of(d)
        remote(qg.at[g], qg.at[g], a_send.at[2, d], q_recv.at[g], group_peer(d)[1]).wait_recv()
    for copy in text_in:
        copy.wait()

    def start_text():
        for h in range(heads):
            s = score(h, tks[h])
            live = lax.broadcasted_iota(jnp.int32, s.shape, 1) < count_ref[0]
            s = jnp.where(live, s, -jnp.inf)
            top = jnp.max(s, axis=1, keepdims=True)
            p = jnp.exp2(s - top)
            peak[h] = top
            total[h] = jnp.sum(p, axis=1, keepdims=True)
            acc[h] = jnp.dot(p.astype(jnp.bfloat16), tvs[h], preferred_element_type=jnp.float32)

    def keys_of(s, h):
        return kv[s, 0, :, h].reshape(rows, dim)

    def values_of(s, h):
        return kv[s, 1, :, h].reshape(rows, dim)

    def weigh(h, keys):
        sc = score(h, keys)
        old = peak[h]
        top = jnp.maximum(old, jnp.max(sc, axis=1, keepdims=True))
        p = jnp.exp2(sc - top)
        factor = jnp.exp2(old - top)
        peak[h] = top
        total[h] = total[h] * factor + jnp.sum(p, axis=1, keepdims=True)
        return p.astype(jnp.bfloat16), factor

    def absorb(s):
        for h in range(heads):
            p, factor = weigh(h, keys_of(s, h))
            acc[h] = acc[h] * factor + jnp.dot(p, values_of(s, h), preferred_element_type=jnp.float32)

    other = near_peer(1)[0]
    near_slot = fi * NEAR + other

    def from_far(i):
        f = far_peer(i + 1)[0]
        return f * NEAR + ni, f * NEAR + other

    def relay(i, w, d):
        s, g = from_far(i)[0], group_of(d)
        arrived(s, w, g)
        kv_to_near(s, w, g, 1).start()

    def take(s, w):
        for d in range(groups):
            arrived(s, w, group_of(d))

    def whole(i):
        for w, d in early + late:
            relay(i, w, d)
        straight, across = from_far(i)
        absorb(straight)
        take(across, 0)
        take(across, 1)
        absorb(across)

    start_text()
    each(far - 2, whole)
    last = far - 2
    straight, across = from_far(last)
    relay(last, 0, 0)
    relay(last, 1, 0)
    absorb(slot)
    for w, d in early[2:]:
        relay(last, w, d)
    take(near_slot, 0)
    take(near_slot, 1)
    absorb(near_slot)
    for w, d in late:
        relay(last, w, d)
    take(across, 0)
    for h in range(heads):
        p, factor = weigh(h, jnp.concatenate([keys_of(straight, h), keys_of(across, h)], axis=0))
        probs[h] = p
        acc[h] = acc[h] * factor
    for h in range(heads):
        acc[h] += jnp.dot(probs[h, :, :rows], values_of(straight, h), preferred_element_type=jnp.float32)
    take(across, 1)

    def out_to(h, d):
        g, peer = group_peer(d)
        return remote(ost.at[h, g], out_ref.at[mine, h], o_send.at[h, d], o_recv.at[h, mine], peer)

    partner = lax.rem(mi + 1, PAIR)

    def text_to(h):
        return remote(tst.at[h, partner], tout_ref.at[mi, h], t_sems.at[0, h], t_sems.at[1, h],
                      at(fi, partner, ni, hd))

    for h in range(heads):
        mixed = acc[h] + jnp.dot(probs[h, :, rows:], values_of(across, h), preferred_element_type=jnp.float32)
        result = (mixed / total[h]).astype(jnp.bfloat16)
        ost[h] = result[:rows].reshape(groups, tokens, dim)
        tst[h] = result[rows:].reshape(tst.shape[1:])
        for d in range(1, groups):
            out_to(h, d).start()
        text_to(h).start()
        out_ref[mine, h] = ost[h, mine]
        tout_ref[mi, h] = tst[h, mi]

    for d in range(1, groups):
        kv_to_group(0, d).wait_send()
        kv_to_group(1, d).wait_send()
        q_to_group(d).wait_send()
    for w in range(2):
        for d in range(groups):
            g = group_of(d)
            each(far - 1, lambda i: kv_to_far(w, g, i + 1).wait_send())
            each(far, lambda i: kv_to_near(far_peer(i)[0] * NEAR + ni, w, g, 1).wait_send())
    for h in range(heads):
        for d in range(1, groups):
            g, peer = group_peer(d)
            out_to(h, d).wait_send()
            remote(ost.at[h, g], out_ref.at[g, h], o_send.at[h, d], o_recv.at[h, g], peer).wait_recv()
        text_to(h).wait_send()
        remote(tst.at[h, partner], tout_ref.at[partner, h], t_sems.at[0, h], t_sems.at[1, h],
               at(fi, partner, ni, hd)).wait_recv()


def settle(out_ref, tout_ref, video_ref, text_ref, sems):
    copies = (
        pltpu.make_async_copy(out_ref, video_ref, sems.at[0]),
        pltpu.make_async_copy(tout_ref, text_ref, sems.at[1]),
    )
    for copy in copies:
        copy.start()
    for copy in copies:
        copy.wait()


def local(ctxs, hds, video_q, video_k, video_v, positions, text_q, text_k, text_v, text_count):
    tokens, all_heads, dim = video_q.shape
    text = text_q.shape[0]
    groups = PAIR * hds
    heads = all_heads // groups
    far = ctxs // (PAIR * NEAR)
    share = text // ctxs
    rows = groups * tokens + PAIR * share
    freq, swap = constants(dim)

    def by_head(x):
        return jnp.swapaxes(x, 0, 1).reshape(groups, heads, tokens, dim)

    vmem = pl.BlockSpec(memory_space=pltpu.VMEM)
    dma = pltpu.SemaphoreType.DMA
    slots = far * NEAR
    out, tout = pl.pallas_call(
        functools.partial(kernel, far, hds),
        name="joint_attention",
        out_shape=(
            pltpu.VMEM((groups, heads, tokens, dim), jnp.bfloat16),
            pltpu.VMEM((PAIR, heads, share, dim), jnp.bfloat16),
        ),
        in_specs=[pl.BlockSpec(memory_space=pl.ANY)] * 9 + [pl.BlockSpec(memory_space=pltpu.SMEM)],
        out_specs=(vmem, vmem),
        scratch_shapes=[
            pltpu.VMEM(positions.shape, jnp.int32),
            pltpu.VMEM((1, dim), jnp.float32),
            pltpu.VMEM((dim, dim), jnp.bfloat16),
            pltpu.VMEM((groups, heads, tokens, dim), jnp.bfloat16),
            pltpu.VMEM((groups, heads, tokens, dim), jnp.bfloat16),
            pltpu.VMEM((heads, ctxs, share, dim), jnp.bfloat16),
            pltpu.VMEM((heads, text, dim), jnp.bfloat16),
            pltpu.VMEM((heads, text, dim), jnp.bfloat16),
            pltpu.VMEM((groups, heads, tokens, dim), jnp.bfloat16),
            pltpu.VMEM((groups, heads, tokens, dim), jnp.bfloat16),
            pltpu.VMEM((groups, heads, tokens, dim), jnp.bfloat16),
            pltpu.VMEM((slots, 2, groups, heads, tokens, dim), jnp.bfloat16),
            pltpu.VMEM((heads, groups, tokens, dim), jnp.bfloat16),
            pltpu.VMEM((heads, PAIR, share, dim), jnp.bfloat16),
            pltpu.VMEM((heads, rows, dim), jnp.float32),
            pltpu.VMEM((heads, rows, 1), jnp.float32),
            pltpu.VMEM((heads, rows, 1), jnp.float32),
            pltpu.VMEM((heads, rows, 2 * groups * tokens), jnp.bfloat16),
            dma((9,)),
            dma((3, groups)),
            dma((groups,)),
            dma((slots, 2, groups)),
            dma((far, 2, groups)),
            dma((far, 2, groups)),
            dma((heads, groups)),
            dma((heads, groups)),
            dma((2, heads)),
        ],
        compiler_params=pltpu.CompilerParams(
            collective_id=0, has_side_effects=True, vmem_limit_bytes=60 * 1024 * 1024
        ),
    )(
        by_head(video_q), by_head(video_k), by_head(video_v),
        jnp.swapaxes(text_q, 0, 1).reshape(PAIR * heads, ctxs, share, dim), jnp.swapaxes(text_k, 0, 1), jnp.swapaxes(text_v, 0, 1),
        positions, jnp.asarray(freq[None, :]), jnp.asarray(swap, jnp.bfloat16), text_count,
    )
    out, tout = pl.pallas_call(
        settle,
        name="settle",
        out_shape=(jax.ShapeDtypeStruct(out.shape, out.dtype), jax.ShapeDtypeStruct(tout.shape, tout.dtype)),
        in_specs=[vmem] * 2,
        out_specs=(pl.BlockSpec(memory_space=pl.ANY),) * 2,
        scratch_shapes=[dma((2,))],
    )(pltpu.with_memory_space_constraint(out, pltpu.VMEM), pltpu.with_memory_space_constraint(tout, pltpu.VMEM))
    video_out = jnp.swapaxes(out.reshape(all_heads, tokens, dim), 0, 1)
    text_out = jnp.swapaxes(tout.reshape(PAIR * heads, share, dim), 0, 1)
    return (video_out, text_out)


def solution(mesh):
    return jax.shard_map(
        functools.partial(local, mesh.shape["ctx"], mesh.shape["hd"]),
        mesh=mesh,
        in_specs=(
            P(("ctx", "hd"), "grp", None),
            P(("ctx", "hd"), "grp", None),
            P(("ctx", "hd"), "grp", None),
            P(None, ("ctx", "hd")),
            P(None, ("grp", "hd"), None),
            P(None, ("grp", "hd"), None),
            P(None, ("grp", "hd"), None),
            P(),
        ),
        out_specs=(P(("ctx", "hd"), "grp", None), P("ctx", ("grp", "hd"), None)),
        check_vma=False,
    )
```

```python
import contextlib
import functools
import math

import jax
import jax.numpy as jnp
import numpy as np
from jax import lax
from jax.experimental import pallas as pl
from jax.experimental.pallas import tpu as pltpu
from jax.sharding import PartitionSpec as P

THETA = 256.0
MESH = pl.DeviceIdType.MESH
NEARS = ('V', 'K')
BESIDE = ('Q', 'V', 'K')
INNER_OWN = ('Vz', 'Kz', 'Qz', 'Vd', 'Kd', 'Qd')
INNER_FAR = ('bVz', 'bKz', 'aKz', 'bVd', 'bKd', 'aKd', 'aV')
OUTER = ('Vz', 'Kz', 'Qz', 'Vd', 'Kd', 'Qd', 'Kn', 'Ka', 'V')
STEPS = ('vz', 'vy', 'bvz', 'ky', 'kz', 'bkz', 'nkz', 'vd', 'bvd', 'kd', 'bkd', 'q', 'nkd', 'fk0', 'ok0', 'fk1', 'fv0', 'ok1', 'ov', 'fv1', 'w0', 'fv2', 'nv0', 'nv1', 'nv2', 'w1', 'f0', 'f1', 'f2')
PAIR = 2
NEAR = 2


def bands(dim):
    band_t = dim // 8
    band_h = (dim - band_t) // 2
    return (band_t, band_h, dim - band_t - band_h)


def constants(dim):
    freq = np.zeros((dim,), np.float32)
    swap = np.zeros((dim, dim), np.float32)
    start = 0
    for size in bands(dim):
        half = size // 2
        for i in range(half):
            low, high = start + i, start + half + i
            freq[low] = freq[high] = np.float32(THETA ** (-2.0 * i / size))
            swap[high, low] = -1.0
            swap[low, high] = 1.0
        start += size
    return freq, swap


def each(count, body):
    if count <= 4:
        for i in range(count):
            body(i)
    else:
        lax.fori_loop(0, count, lambda i, _: (body(i), 0)[1], 0)


def mark(name):
    return contextlib.nullcontext()


def far_items(heads):
    return [(0, 0, 1)] + [(0, 1, heads)] * (heads > 1) + [(1, h, h + 1) for h in range(heads)]


def kernel(cores, far, hds, q_ref, k_ref, v_ref, tq_ref, tk_ref, tv_ref, pos_in, freq_in, swap_in, count_ref,
           out_ref, tout_ref, pos_ref, freq_ref, swap_ref, qin, kin, tqs, tks, tvs, qs, ks, qg, kv, ost, tst, acc, peak, total, held, probs,
           in_sems, own_recv, far_recv, far_across, bulk_recv, bulk_across, once):
    ctx = lax.axis_index("ctx")
    hd = lax.axis_index("hd")
    fi, mi, ni = ctx // (PAIR * NEAR), (ctx // NEAR) % PAIR, ctx % NEAR
    groups = PAIR * hds
    heads = v_ref.shape[1]
    tokens, dim = v_ref.shape[2], v_ref.shape[3]
    other = lax.rem(ni + 1, NEAR)
    mine = hd * PAIR + mi
    place = mi * hds + hd
    own_items = [(1, 0, heads), (0, 0, heads)]
    items = far_items(heads)
    inner = lax.rem(fi + mi, 2) == 1
    q_send, q_recv, own_send, own_pass, v_across, k_across, far_send, far_pass, o_send, o_recv, t_send, t_recv = (
        once.at[i] for i in range(12))
    own_across = (v_across, k_across)

    def at(f, m, n, h):
        return {"ctx": (f * PAIR + m) * NEAR + n, "hd": h}

    near = at(fi, mi, other, hd)
    offsets = [(0, dh) for dh in range(1, hds)] + [(dm, dh) for dm in range(1, PAIR) for dh in range(hds)]

    def mate(dm, dh):
        return lax.rem(mi + dm, PAIR), lax.rem(hd + dh, hds)

    def far_of(i):
        return lax.rem(fi + i, far)

    def side(f, outward):
        return lax.rem(f + 1 + outward, PAIR)

    text_heads = pl.ds(mi * heads, heads)
    k_in = pltpu.make_async_copy(k_ref, kin, in_sems.at[0])
    q_in = pltpu.make_async_copy(q_ref, qin, in_sems.at[1])
    v_in = pltpu.make_async_copy(v_ref.at[mine], kv.at[ni, 1, :, fi * groups + place], in_sems.at[2])
    text_in = tuple(
        pltpu.make_async_copy(tq_ref.at[text_heads, (fi * PAIR + m) * NEAR + ni], tqs.at[:, m], in_sems.at[8 + m])
        for m in range(PAIR)
    ) + (
        pltpu.make_async_copy(tk_ref.at[text_heads], tks, in_sems.at[3]),
        pltpu.make_async_copy(tv_ref.at[text_heads], tvs, in_sems.at[4]),
    )
    table_in = (
        pltpu.make_async_copy(pos_in, pos_ref, in_sems.at[5]),
        pltpu.make_async_copy(freq_in, freq_ref, in_sems.at[6]),
        pltpu.make_async_copy(swap_in, swap_ref, in_sems.at[7]),
    )
    barrier = pltpu.get_barrier_semaphore()

    def greet(peer):
        for g in range(cores):
            pl.semaphore_signal(barrier, inc=1, device_id=dict(peer, grp=g), device_id_type=MESH)

    def greet_far(i):
        for m in range(PAIR):
            for h in range(hds):
                greet(at(far_of(i + 1), m, ni, h))

    each(far - 1, greet_far)
    for dm, dh in offsets:
        m, h = mate(dm, dh)
        greet(at(fi, m, ni, h))
    greet(near)
    for copy in table_in + (k_in, q_in, v_in) + text_in:
        copy.start()
    with mark("tablewait"):
        for copy in table_in:
            copy.wait()
    swap = swap_ref[...]
    diagonal = (lax.broadcasted_iota(jnp.int32, (tokens, tokens), 0)
                == lax.broadcasted_iota(jnp.int32, (tokens, tokens), 1))
    lane = lax.broadcasted_iota(jnp.int32, (tokens, dim), 1)

    def column(axis):
        row = pos_ref[axis:axis + 1, :].astype(jnp.float32)
        return jnp.sum(jnp.where(diagonal, row, 0.0), axis=1, keepdims=True)

    band_t, band_h, _ = bands(dim)
    angle = jnp.where(lane < band_t, column(0), jnp.where(lane < band_t + band_h, column(1), column(2))) * freq_ref[...]
    cos, sin = jnp.cos(angle), jnp.sin(angle)

    def rotate(src, dst):
        for g in range(groups):
            for h in range(heads):
                x = src[g, h]
                turned = jnp.dot(x, swap, preferred_element_type=jnp.float32)
                dst[g, h] = (x.astype(jnp.float32) * cos + turned * sin).astype(jnp.bfloat16)

    with mark("rot"):
        k_in.wait()
        rotate(kin, ks)
        q_in.wait()
        rotate(qin, qs)
    with mark("barrier"):
        pl.semaphore_wait(barrier, cores * ((groups - 1) + (far - 1) * groups + 1))

    def remote(src, dst, send, recv, peer):
        return pltpu.make_async_remote_copy(src_ref=src, dst_ref=dst, send_sem=send, recv_sem=recv,
                                            device_id=peer, device_id_type=MESH)

    def received(ref, sem):
        remote(ref, ref, own_send, sem, near).wait_recv()

    def left(ref, sem):
        remote(ref, ref, sem, v_across, near).wait_send()

    def source(w, g, lo, hi):
        return (ks if w == 0 else v_ref).at[g, pl.ds(lo, hi - lo)]

    def part(n, w, lo, hi, s, count=None):
        return kv.at[n, w, pl.ds(lo, hi - lo), s if count is None else pl.ds(s, count)]

    me = fi * groups + place

    def own_to_mate(j, dm, dh):
        w, lo, hi = own_items[j]
        m, h = mate(dm, dh)
        return remote(source(w, h * PAIR + m, lo, hi), part(ni, w, lo, hi, me), own_send, own_recv.at[j, dm, dh], at(fi, m, ni, h))

    def mine_to_near(j):
        w, lo, hi = own_items[j]
        return remote(source(w, mine, lo, hi), part(ni, w, lo, hi, me), own_send, own_across[j], near)

    def pass_on(block, arrive, send, across):
        received(block, arrive)
        remote(block, block, send, across, near).start()

    def own_relay(j, dm, dh):
        w, lo, hi = own_items[j]
        m, h = lax.rem(mi + PAIR - dm, PAIR), lax.rem(hd + hds - dh, hds)
        pass_on(part(ni, w, lo, hi, fi * groups + m * hds + h), own_recv.at[j, dm, dh], own_pass, own_across[j])

    def far_send_one(j, i, outward, dhs):
        w, lo, hi = items[j] if j >= 0 else (j + 2, 0, heads)
        f = far_of(i)
        m = side(f, outward)
        for dh in dhs:
            h = lax.rem(hd + dh, hds)
            arrive = far_recv.at[j, far - i - 1, mi, dh] if j >= 0 else bulk_recv.at[j + 2, far - i - 1, dh]
            remote(source(w, h * PAIR + m, lo, hi), part(ni, w, lo, hi, me), far_send, arrive,
                   at(f, m, ni, h)).start()

    def far_sends(order):
        def send(i):
            for j, outward, dhs in order:
                far_send_one(j, i + 1, outward, dhs)

        each(far - 1, send)

    def relay(i, j, outward, dhs):
        w, lo, hi = items[j]
        f = far_of(i)
        m = side(f, outward)
        for dh in dhs:
            pass_on(part(ni, w, lo, hi, f * groups + m * hds + lax.rem(hd + hds - dh, hds)), far_recv.at[j, i - 1, m, dh],
                    far_pass, far_across.at[j, i - 1])

    def take(i, j):
        w, lo, hi = items[j]

        @pl.when(inner)
        def _():
            received(part(other, w, lo, hi, far_of(i) * groups, hds), far_across.at[j, i - 1])

        @pl.when(jnp.logical_not(inner))
        def _():
            received(part(other, w, lo, hi, far_of(i) * groups, groups), far_across.at[j, i - 1])

    def relay_bulk(i, w, dhs):
        f = far_of(i)
        for dh in dhs:
            pass_on(part(ni, w, 0, heads, f * groups + side(f, 0) * hds + lax.rem(hd + hds - dh, hds)),
                    bulk_recv.at[w, i - 1, dh], far_pass, bulk_across.at[w, i - 1])

    def take_bulk(i, w):
        @pl.when(inner)
        def _():
            received(part(other, w, 0, heads, far_of(i) * groups, hds), bulk_across.at[w, i - 1])

    def by_place(near_side, far_side):
        @pl.when(inner)
        def _():
            near_side()

        @pl.when(jnp.logical_not(inner))
        def _():
            far_side()

    def q_to_mate(dm, dh):
        m, h = mate(dm, dh)
        return remote(qs.at[h * PAIR + m], qg.at[place], q_send, q_recv, at(fi, m, ni, h))

    beside = [(0, dh) for dh in range(1, hds)]
    ahead = [(dm, 0) for dm in range(1, PAIR)]
    askew = [(dm, dh) for dm in range(1, PAIR) for dh in range(1, hds)]
    straight, skew, both = (0,), tuple(range(1, hds)), tuple(range(hds))

    def own_sends(j, which):
        for dm, dh in which:
            own_to_mate(j, dm, dh).start()

    def q_sends(which):
        for dm, dh in which:
            q_to_mate(dm, dh).start()


    k_items = [j for j, item in enumerate(items) if item[0] == 0]
    v_items = [j for j, item in enumerate(items) if item[0] == 1]
    sends = {
        "Vz": lambda: own_sends(0, ahead),
        "Kz": lambda: own_sends(1, ahead),
        "Kd": lambda: own_sends(1, askew),
        "Vd": lambda: own_sends(0, askew),
        "Qz": lambda: q_sends(ahead),
        "Qd": lambda: q_sends(askew),
        "bVz": lambda: far_sends([(-1, 0, straight)]),
        "bKz": lambda: far_sends([(-2, 0, straight)]),
        "bKd": lambda: far_sends([(-2, 0, skew)]),
        "bVd": lambda: far_sends([(-1, 0, skew)]),
        "aKz": lambda: far_sends([(j, 1, straight) for j in k_items]),
        "aKd": lambda: far_sends([(j, 1, skew) for j in k_items]),
        "aV": lambda: far_sends([(j, 1, both) for j in v_items]),
        "aV0": lambda: far_sends([(j, 1, both) for j in v_items[:1]]),
        "aV1": lambda: far_sends([(j, 1, both) for j in v_items[1:]]),
        "V0": lambda: far_sends([(j, o, both) for j in v_items[:1] for o in (0, 1)]),
        "V1": lambda: far_sends([(j, o, both) for j in v_items[1:] for o in (0, 1)]),
        "aVz": lambda: far_sends([(j, 1, straight) for j in v_items]),
        "aVd": lambda: far_sends([(j, 1, skew) for j in v_items]),
        "K": lambda: far_sends([(j, o, both) for j in k_items for o in (0, 1)]),
        "Kn": lambda: far_sends([(j, 0, both) for j in k_items]),
        "Ka": lambda: far_sends([(j, 1, both) for j in k_items]),
        "V": lambda: far_sends([(j, o, both) for j in v_items for o in (0, 1)]),
        "W": lambda: far_sends([(j, o, both) for j in v_items for o in (1, 0)]),
        "Vn": lambda: far_sends([(j, 0, both) for j in v_items]),
        "Va": lambda: far_sends([(j, 1, both) for j in v_items]),
    }

    def issue(names):
        for name in names:
            sends[name]()

    kinds = ("V", "K")
    for name in NEARS:
        mine_to_near(kinds.index(name)).start()
    for name in BESIDE:
        if name == "Q":
            q_sends(beside)
        else:
            own_sends(kinds.index(name), beside)
    by_place(lambda: issue(INNER_OWN + INNER_FAR), lambda: issue(OUTER))

    for h in range(heads):
        kv[ni, 0, h, me] = ks[mine, h]
    qg[place] = qs[mine]
    v_in.wait()

    scale = math.log2(math.e) / math.sqrt(dim)
    rows = groups * tokens

    def queries(h):
        own_text = [tqs[h, m] for m in range(PAIR)]
        return jnp.concatenate([qg[:, h].reshape(rows, dim)] + own_text, axis=0)

    def score(h, keys):
        return lax.dot_general(queries(h), keys, (((1,), (1,)), ((), ())), preferred_element_type=jnp.float32) * scale

    def block(w, n, f, h):
        return kv[n, w, h, pl.ds(f * groups, groups)].reshape(rows, dim)

    def weigh(f, h):
        sc = score(h, jnp.concatenate([block(0, ni, f, h), block(0, other, f, h)], axis=0))
        old = peak[h]
        top = jnp.maximum(old, jnp.max(sc, axis=1, keepdims=True))
        p = jnp.exp2(sc - top)
        factor = jnp.exp2(old - top)
        peak[h] = top
        total[h] = total[h] * factor + jnp.sum(p, axis=1, keepdims=True)
        acc[h] = acc[h] * factor
        return p.astype(jnp.bfloat16)

    def values(f, h):
        return jnp.concatenate([block(1, ni, f, h), block(1, other, f, h)], axis=0)

    def absorb(f, h):
        p = weigh(f, h)
        acc[h] += jnp.dot(p, values(f, h), preferred_element_type=jnp.float32)

    last = far - 1
    f_last = far_of(last)

    def from_inner(js, dhs):
        def go():
            for j in js:
                relay(last, j, 0, dhs)

        pl.when(jnp.logical_not(inner))(go)

    def whole(i):
        def fetch(order):
            for j in range(len(items)):
                for outward in order:
                    relay(i + 1, j, outward, both)

        def bulk():
            relay_bulk(i + 1, 1, both)
            relay_bulk(i + 1, 0, both)
            fetch((1,))

        by_place(bulk, lambda: fetch((0, 1)))
        for w in range(2):
            take_bulk(i + 1, w)
        for j in range(len(items)):
            take(i + 1, j)
        for h in range(heads):
            absorb(far_of(i + 1), h)

    def queries_in():
        with mark("qwait"):
            received(qg.at[pl.ds(0, groups - 1)], q_recv)
            for copy in text_in:
                copy.wait()
        with mark("text"):
            for h in range(heads):
                s = score(h, tks[h])
                live = lax.broadcasted_iota(jnp.int32, s.shape, 1) < count_ref[0]
                s = jnp.where(live, s, -jnp.inf)
                top = jnp.max(s, axis=1, keepdims=True)
                p = jnp.exp2(s - top)
                peak[h] = top
                total[h] = jnp.sum(p, axis=1, keepdims=True)
                acc[h] = jnp.dot(p.astype(jnp.bfloat16), tvs[h], preferred_element_type=jnp.float32)
        each(far - 2, whole)

    partner = lax.rem(mi + 1, PAIR)

    def finish(h):
        acc[h] += jnp.dot(probs[h, :, :rows], block(1, ni, f_last, h), preferred_element_type=jnp.float32)
        mixed = acc[h] + jnp.dot(probs[h, :, rows:], block(1, other, f_last, h), preferred_element_type=jnp.float32)
        result = (mixed / total[h]).astype(jnp.bfloat16)
        ost[h] = result[:rows].reshape(groups, tokens, dim)
        tst[h] = result[rows:].reshape(tst.shape[1:])
        for dm, dh in reversed(offsets):
            m, h2 = mate(dm, dh)
            remote(ost.at[h, m * hds + h2], out_ref.at[mine, h], o_send, o_recv, at(fi, m, ni, h2)).start()
        remote(tst.at[h, partner], tout_ref.at[mi, h], t_send, t_recv, at(fi, partner, ni, hd)).start()
        out_ref[mine, h] = ost[h, place]
        tout_ref[mi, h] = tst[h, mi]

    def own_step(j, which):
        def go():
            for dm, dh in which:
                own_relay(j, dm, dh)

        return go

    def at_inner(w, dhs):
        return lambda: pl.when(inner)(lambda: relay_bulk(last, w, dhs))

    def away(js):
        def go():
            for j in js:
                relay(last, j, 1, both)

        return go

    def per_head(lo, body):
        def go(h, _):
            body(h)
            return 0

        lax.fori_loop(lo, heads, go, 0)

    def own_weigh(h):
        held[h] = weigh(fi, h)

    def far_weigh(h):
        probs[h] = weigh(f_last, h)

    def own_mix(h):
        acc[h] += jnp.dot(held[h], values(fi, h), preferred_element_type=jnp.float32)

    def own_first():
        received(kv.at[other, 0, :, pl.ds(fi * groups, groups)], k_across)
        own_weigh(0)

    def own_values():
        received(kv.at[other, 1, :, pl.ds(fi * groups, groups)], v_across)
        per_head(0, own_mix)

    def far_first():
        take_bulk(last, 0)
        take(last, 0)
        far_weigh(0)

    def far_rest():
        for j in k_items[1:]:
            take(last, j)
        per_head(1, far_weigh)

    def finish_first():
        take_bulk(last, 1)
        take(last, v_items[0])
        finish(0)

    def finish_heads(hs):
        def go():
            for h in hs:
                take(last, v_items[h])
                finish(h)

        return go

    steps = {
        "vy": own_step(0, beside),
        "vz": own_step(0, ahead),
        "vd": own_step(0, askew),
        "ky": own_step(1, beside),
        "kz": own_step(1, ahead),
        "kd": own_step(1, askew),
        "bvz": at_inner(1, straight),
        "bvd": at_inner(1, skew),
        "bkz": at_inner(0, straight),
        "bkd": at_inner(0, skew),
        "nkz": lambda: from_inner(k_items, straight),
        "nkd": lambda: from_inner(k_items, skew),
        "nv0": lambda: from_inner(v_items[:1], both),
        "nv1": lambda: from_inner(v_items[1:2], both),
        "nv2": lambda: from_inner(v_items[2:], both),
        "fk0": away(k_items[:1]),
        "fk1": away(k_items[1:]),
        "fv0": away(v_items[:1]),
        "fv1": away(v_items[1:2]),
        "fv2": away(v_items[2:]),
        "q": queries_in,
        "ok0": own_first,
        "ok1": lambda: per_head(1, own_weigh),
        "ov": own_values,
        "w0": far_first,
        "w1": far_rest,
        "f0": finish_first,
        "f1": finish_heads(range(1, min(2, heads))),
        "f2": finish_heads(range(2, heads)),
    }
    for name in STEPS:
        with mark(name):
            steps[name]()

    with mark("sent"):
        every = kv.at[ni, :, :, pl.ds(0, groups)]
        left(every, own_send)
        left(kv.at[ni, :, :, pl.ds(0, groups - 1)], own_pass)
        left(kv.at[ni, :, :, pl.ds(0, (far - 1) * groups)], far_send)
        left(kv.at[ni, :, :, pl.ds(0, (far - 1) * groups)], far_pass)
        left(qs.at[pl.ds(0, groups - 1)], q_send)
        left(ost.at[:, pl.ds(0, groups - 1)], o_send)
        left(tst.at[:, 0], t_send)
    with mark("outwait"):
        received(ost.at[:, pl.ds(0, groups - 1)], o_recv)
        received(tst.at[:, 0], t_recv)


def settle(out_ref, tout_ref, video_ref, text_ref, sems):
    copies = (
        pltpu.make_async_copy(out_ref, video_ref, sems.at[0]),
        pltpu.make_async_copy(tout_ref, text_ref, sems.at[1]),
    )
    for copy in copies:
        copy.start()
    for copy in copies:
        copy.wait()


def local(cores, ctxs, hds, video_q, video_k, video_v, positions, text_q, text_k, text_v, text_count):
    tokens, all_heads, dim = video_q.shape
    text = text_q.shape[0]
    groups = PAIR * hds
    heads = all_heads // groups
    far = ctxs // (PAIR * NEAR)
    share = text // ctxs
    rows = groups * tokens + PAIR * share
    freq, swap = constants(dim)

    def by_head(x):
        return jnp.swapaxes(x, 0, 1).reshape(groups, heads, tokens, dim)

    vmem = pl.BlockSpec(memory_space=pltpu.VMEM)
    dma = pltpu.SemaphoreType.DMA
    count = len(far_items(heads))
    out, tout = pl.pallas_call(
        functools.partial(kernel, cores, far, hds),
        name="joint_attention",
        out_shape=(
            pltpu.VMEM((groups, heads, tokens, dim), jnp.bfloat16),
            pltpu.VMEM((PAIR, heads, share, dim), jnp.bfloat16),
        ),
        in_specs=[pl.BlockSpec(memory_space=pl.ANY)] * 9 + [pl.BlockSpec(memory_space=pltpu.SMEM)],
        out_specs=(vmem, vmem),
        scratch_shapes=[
            pltpu.VMEM(positions.shape, jnp.int32),
            pltpu.VMEM((1, dim), jnp.float32),
            pltpu.VMEM((dim, dim), jnp.bfloat16),
            pltpu.VMEM((groups, heads, tokens, dim), jnp.bfloat16),
            pltpu.VMEM((groups, heads, tokens, dim), jnp.bfloat16),
            pltpu.VMEM((heads, PAIR, share, dim), jnp.bfloat16),
            pltpu.VMEM((heads, text, dim), jnp.bfloat16),
            pltpu.VMEM((heads, text, dim), jnp.bfloat16),
            pltpu.VMEM((groups, heads, tokens, dim), jnp.bfloat16),
            pltpu.VMEM((groups, heads, tokens, dim), jnp.bfloat16),
            pltpu.VMEM((groups, heads, tokens, dim), jnp.bfloat16),
            pltpu.VMEM((NEAR, 2, heads, far * groups, tokens, dim), jnp.bfloat16),
            pltpu.VMEM((heads, groups, tokens, dim), jnp.bfloat16),
            pltpu.VMEM((heads, PAIR, share, dim), jnp.bfloat16),
            pltpu.VMEM((heads, rows, dim), jnp.float32),
            pltpu.VMEM((heads, rows, 1), jnp.float32),
            pltpu.VMEM((heads, rows, 1), jnp.float32),
            pltpu.VMEM((heads, rows, 2 * groups * tokens), jnp.bfloat16),
            pltpu.VMEM((heads, rows, 2 * groups * tokens), jnp.bfloat16),
            dma((8 + PAIR,)),
            dma((2, PAIR, hds)),
            dma((count, far - 1, PAIR, hds)),
            dma((count, far - 1)),
            dma((2, far - 1, hds)),
            dma((2, far - 1)),
            dma((12,)),
        ],
        compiler_params=pltpu.CompilerParams(
            collective_id=0, has_side_effects=True, vmem_limit_bytes=60 * 1024 * 1024
        ),
    )(
        by_head(video_q), by_head(video_k), by_head(video_v),
        jnp.swapaxes(text_q, 0, 1).reshape(PAIR * heads, ctxs, share, dim), jnp.swapaxes(text_k, 0, 1), jnp.swapaxes(text_v, 0, 1),
        positions, jnp.asarray(freq[None, :]), jnp.asarray(swap, jnp.bfloat16), text_count,
    )
    out, tout = pl.pallas_call(
        settle,
        name="settle",
        out_shape=(jax.ShapeDtypeStruct(out.shape, out.dtype), jax.ShapeDtypeStruct(tout.shape, tout.dtype)),
        in_specs=[vmem] * 2,
        out_specs=(pl.BlockSpec(memory_space=pl.ANY),) * 2,
        scratch_shapes=[dma((2,))],
    )(pltpu.with_memory_space_constraint(out, pltpu.VMEM), pltpu.with_memory_space_constraint(tout, pltpu.VMEM))
    video_out = jnp.swapaxes(out.reshape(all_heads, tokens, dim), 0, 1)
    text_out = jnp.swapaxes(tout.reshape(PAIR * heads, share, dim), 0, 1)
    return (video_out, text_out)


def solution(mesh):
    return jax.shard_map(
        functools.partial(local, mesh.shape["grp"], mesh.shape["ctx"], mesh.shape["hd"]),
        mesh=mesh,
        in_specs=(
            P(("ctx", "hd"), "grp", None),
            P(("ctx", "hd"), "grp", None),
            P(("ctx", "hd"), "grp", None),
            P(None, ("ctx", "hd")),
            P(None, ("grp", "hd"), None),
            P(None, ("grp", "hd"), None),
            P(None, ("grp", "hd"), None),
            P(),
        ),
        out_specs=(P(("ctx", "hd"), "grp", None), P("ctx", ("grp", "hd"), None)),
        check_vma=False,
    )
```

```python
import contextlib
import functools
import math

import jax
import jax.numpy as jnp
import numpy as np
from jax import lax
from jax.experimental import pallas as pl
from jax.experimental.pallas import tpu as pltpu
from jax.sharding import PartitionSpec as P

THETA = 256.0
MESH = pl.DeviceIdType.MESH
NEARS = ('V', 'K')
BESIDE = ('Q', 'V', 'K')
INNER_OWN = ('Vz', 'Qz', 'Kz', 'Vd', 'Kd', 'Qd')
INNER_FAR = ('bVz', 'bKz', 'aKz', 'bVd', 'bKd', 'aKd', 'aV')
OUTER = ('Vz', 'Kz', 'Qz', 'Vd', 'Kd', 'Qd', 'Kn', 'Ka', 'V')
STEPS = ('vz', 'vy', 'bvz', 'ky', 'kz', 'bkz', 'nkz', 'vd', 'bvd', 'kd', 'bkd', 'q', 'nkd', 'fk0', 'ok0', 'fk1', 'fv0', 'ok1', 'ov', 'fv1', 'w0', 'fv2', 'nv0', 'nv1', 'nv2', 'w1', 'f0', 'f1', 'f2')
PAIR = 2
NEAR = 2


def bands(dim):
    band_t = dim // 8
    band_h = (dim - band_t) // 2
    return (band_t, band_h, dim - band_t - band_h)


def constants(dim):
    freq = np.zeros((dim,), np.float32)
    swap = np.zeros((dim, dim), np.float32)
    start = 0
    for size in bands(dim):
        half = size // 2
        for i in range(half):
            low, high = start + i, start + half + i
            freq[low] = freq[high] = np.float32(THETA ** (-2.0 * i / size))
            swap[high, low] = -1.0
            swap[low, high] = 1.0
        start += size
    return freq, swap


def each(count, body):
    if count <= 4:
        for i in range(count):
            body(i)
    else:
        lax.fori_loop(0, count, lambda i, _: (body(i), 0)[1], 0)


def mark(name):
    return contextlib.nullcontext()


def far_items(heads):
    return [(0, 0, heads)] + [(1, h, h + 1) for h in range(heads)]


def kernel(cores, far, hds, q_ref, k_ref, v_ref, tq_ref, tk_ref, tv_ref, pos_in, freq_in, swap_in, count_ref,
           out_ref, tout_ref, pos_ref, freq_ref, swap_ref, qin, kin, tqs, tks, tvs, qs, ks, qg, kv, ost, tst, acc, peak, total, held, probs,
           in_sems, own_recv, far_recv, far_across, bulk_recv, bulk_across, once):
    ctx = lax.axis_index("ctx")
    hd = lax.axis_index("hd")
    fi, mi, ni = ctx // (PAIR * NEAR), (ctx // NEAR) % PAIR, ctx % NEAR
    groups = PAIR * hds
    heads = v_ref.shape[1]
    tokens, dim = v_ref.shape[2], v_ref.shape[3]
    other = lax.rem(ni + 1, NEAR)
    mine = hd * PAIR + mi
    place = mi * hds + hd
    own_items = [(1, 0, heads), (0, 0, heads)]
    items = far_items(heads)
    inner = lax.rem(fi + mi, 2) == 1
    q_send, q_recv, own_send, own_pass, v_across, k_across, o_send, o_recv, t_send, t_recv = (
        once.at[i] for i in range(10))
    own_across = (v_across, k_across)

    def at(f, m, n, h):
        return {"ctx": (f * PAIR + m) * NEAR + n, "hd": h}

    near = at(fi, mi, other, hd)
    offsets = [(0, dh) for dh in range(1, hds)] + [(dm, dh) for dm in range(1, PAIR) for dh in range(hds)]

    def mate(dm, dh):
        return lax.rem(mi + dm, PAIR), lax.rem(hd + dh, hds)

    def far_of(i):
        return lax.rem(fi + i, far)

    def side(f, outward):
        return lax.rem(f + 1 + outward, PAIR)

    text_heads = pl.ds(mi * heads, heads)
    k_in = pltpu.make_async_copy(k_ref, kin, in_sems.at[0])
    q_in = pltpu.make_async_copy(q_ref, qin, in_sems.at[1])
    v_in = pltpu.make_async_copy(v_ref.at[mine], kv.at[ni, 1, :, fi * groups + place], in_sems.at[2])
    text_in = tuple(
        pltpu.make_async_copy(tq_ref.at[text_heads, (fi * PAIR + m) * NEAR + ni], tqs.at[:, m], in_sems.at[8 + m])
        for m in range(PAIR)
    ) + (
        pltpu.make_async_copy(tk_ref.at[text_heads], tks, in_sems.at[3]),
        pltpu.make_async_copy(tv_ref.at[text_heads], tvs, in_sems.at[4]),
    )
    table_in = (
        pltpu.make_async_copy(pos_in, pos_ref, in_sems.at[5]),
        pltpu.make_async_copy(freq_in, freq_ref, in_sems.at[6]),
        pltpu.make_async_copy(swap_in, swap_ref, in_sems.at[7]),
    )
    barrier = pltpu.get_barrier_semaphore()

    def greet(peer):
        for g in range(cores):
            pl.semaphore_signal(barrier, inc=1, device_id=dict(peer, grp=g), device_id_type=MESH)

    def greet_far(i):
        for m in range(PAIR):
            for h in range(hds):
                greet(at(far_of(i + 1), m, ni, h))

    each(far - 1, greet_far)
    for dm, dh in offsets:
        m, h = mate(dm, dh)
        greet(at(fi, m, ni, h))
    greet(near)
    for copy in table_in + (k_in, q_in, v_in) + text_in:
        copy.start()
    with mark("tablewait"):
        for copy in table_in:
            copy.wait()
    swap = swap_ref[...]
    diagonal = (lax.broadcasted_iota(jnp.int32, (tokens, tokens), 0)
                == lax.broadcasted_iota(jnp.int32, (tokens, tokens), 1))
    lane = lax.broadcasted_iota(jnp.int32, (tokens, dim), 1)

    def column(axis):
        row = pos_ref[axis:axis + 1, :].astype(jnp.float32)
        return jnp.sum(jnp.where(diagonal, row, 0.0), axis=1, keepdims=True)

    band_t, band_h, _ = bands(dim)
    angle = jnp.where(lane < band_t, column(0), jnp.where(lane < band_t + band_h, column(1), column(2))) * freq_ref[...]
    cos, sin = jnp.cos(angle), jnp.sin(angle)

    def rotate(src, dst):
        for g in range(groups):
            for h in range(heads):
                x = src[g, h]
                turned = jnp.dot(x, swap, preferred_element_type=jnp.float32)
                dst[g, h] = (x.astype(jnp.float32) * cos + turned * sin).astype(jnp.bfloat16)

    with mark("rot"):
        k_in.wait()
        rotate(kin, ks)
        q_in.wait()
        rotate(qin, qs)
    with mark("barrier"):
        pl.semaphore_wait(barrier, cores * ((groups - 1) + (far - 1) * groups + 1))

    def remote(src, dst, send, recv, peer):
        return pltpu.make_async_remote_copy(src_ref=src, dst_ref=dst, send_sem=send, recv_sem=recv,
                                            device_id=peer, device_id_type=MESH)

    def received(ref, sem):
        remote(ref, ref, own_send, sem, near).wait_recv()

    def left(ref, sem):
        remote(ref, ref, sem, v_across, near).wait_send()

    def source(w, g, lo, hi):
        return (ks if w == 0 else v_ref).at[g, pl.ds(lo, hi - lo)]

    def part(n, w, lo, hi, s, count=None):
        return kv.at[n, w, pl.ds(lo, hi - lo), s if count is None else pl.ds(s, count)]

    me = fi * groups + place

    def own_to_mate(j, dm, dh):
        w, lo, hi = own_items[j]
        m, h = mate(dm, dh)
        return remote(source(w, h * PAIR + m, lo, hi), part(ni, w, lo, hi, me), own_send, own_recv.at[j, dm, dh], at(fi, m, ni, h))

    def mine_to_near(j):
        w, lo, hi = own_items[j]
        return remote(source(w, mine, lo, hi), part(ni, w, lo, hi, me), own_send, own_across[j], near)

    def pass_on(block, arrive, send, across):
        received(block, arrive)
        remote(block, block, send, across, near).start()

    def own_relay(j, dm, dh):
        w, lo, hi = own_items[j]
        m, h = lax.rem(mi + PAIR - dm, PAIR), lax.rem(hd + hds - dh, hds)
        pass_on(part(ni, w, lo, hi, fi * groups + m * hds + h), own_recv.at[j, dm, dh], own_pass, own_across[j])

    def far_send_one(j, i, outward, dhs):
        w, lo, hi = items[j] if j >= 0 else (j + 2, 0, heads)
        f = far_of(i)
        m = side(f, outward)
        for dh in dhs:
            h = lax.rem(hd + dh, hds)
            arrive = far_recv.at[j, far - i - 1, mi, dh] if j >= 0 else bulk_recv.at[j + 2, far - i - 1, dh]
            remote(source(w, h * PAIR + m, lo, hi), part(ni, w, lo, hi, me), own_send, arrive,
                   at(f, m, ni, h)).start()

    def far_sends(order):
        def send(i):
            for j, outward, dhs in order:
                far_send_one(j, i + 1, outward, dhs)

        each(far - 1, send)

    def relay(i, j, outward, dhs):
        w, lo, hi = items[j]
        f = far_of(i)
        m = side(f, outward)
        for dh in dhs:
            pass_on(part(ni, w, lo, hi, f * groups + m * hds + lax.rem(hd + hds - dh, hds)), far_recv.at[j, i - 1, m, dh],
                    own_pass, far_across.at[j, i - 1])

    def take(i, j):
        w, lo, hi = items[j]

        @pl.when(inner)
        def _():
            received(part(other, w, lo, hi, far_of(i) * groups, hds), far_across.at[j, i - 1])

        @pl.when(jnp.logical_not(inner))
        def _():
            received(part(other, w, lo, hi, far_of(i) * groups, groups), far_across.at[j, i - 1])

    def relay_bulk(i, w, dhs):
        f = far_of(i)
        for dh in dhs:
            pass_on(part(ni, w, 0, heads, f * groups + side(f, 0) * hds + lax.rem(hd + hds - dh, hds)),
                    bulk_recv.at[w, i - 1, dh], own_pass, bulk_across.at[w, i - 1])

    def take_bulk(i, w):
        @pl.when(inner)
        def _():
            received(part(other, w, 0, heads, far_of(i) * groups, hds), bulk_across.at[w, i - 1])

    def by_place(near_side, far_side):
        @pl.when(inner)
        def _():
            near_side()

        @pl.when(jnp.logical_not(inner))
        def _():
            far_side()

    def q_to_mate(dm, dh):
        m, h = mate(dm, dh)
        return remote(qs.at[h * PAIR + m], qg.at[place], q_send, q_recv, at(fi, m, ni, h))

    beside = [(0, dh) for dh in range(1, hds)]
    ahead = [(dm, 0) for dm in range(1, PAIR)]
    askew = [(dm, dh) for dm in range(1, PAIR) for dh in range(1, hds)]
    straight, skew, both = (0,), tuple(range(1, hds)), tuple(range(hds))

    def own_sends(j, which):
        for dm, dh in which:
            own_to_mate(j, dm, dh).start()

    def q_sends(which):
        for dm, dh in which:
            q_to_mate(dm, dh).start()


    k_items = [j for j, item in enumerate(items) if item[0] == 0]
    v_items = [j for j, item in enumerate(items) if item[0] == 1]
    sends = {
        "Vz": lambda: own_sends(0, ahead),
        "Kz": lambda: own_sends(1, ahead),
        "Kd": lambda: own_sends(1, askew),
        "Vd": lambda: own_sends(0, askew),
        "Qz": lambda: q_sends(ahead),
        "Qd": lambda: q_sends(askew),
        "bVz": lambda: far_sends([(-1, 0, straight)]),
        "bKz": lambda: far_sends([(-2, 0, straight)]),
        "bKd": lambda: far_sends([(-2, 0, skew)]),
        "bVd": lambda: far_sends([(-1, 0, skew)]),
        "aKz": lambda: far_sends([(j, 1, straight) for j in k_items]),
        "aKd": lambda: far_sends([(j, 1, skew) for j in k_items]),
        "aV": lambda: far_sends([(j, 1, both) for j in v_items]),
        "aV0": lambda: far_sends([(j, 1, both) for j in v_items[:1]]),
        "aV1": lambda: far_sends([(j, 1, both) for j in v_items[1:]]),
        "V0": lambda: far_sends([(j, o, both) for j in v_items[:1] for o in (0, 1)]),
        "V1": lambda: far_sends([(j, o, both) for j in v_items[1:] for o in (0, 1)]),
        "aVz": lambda: far_sends([(j, 1, straight) for j in v_items]),
        "aVd": lambda: far_sends([(j, 1, skew) for j in v_items]),
        "K": lambda: far_sends([(j, o, both) for j in k_items for o in (0, 1)]),
        "Kn": lambda: far_sends([(j, 0, both) for j in k_items]),
        "Ka": lambda: far_sends([(j, 1, both) for j in k_items]),
        "V": lambda: far_sends([(j, o, both) for j in v_items for o in (0, 1)]),
        "W": lambda: far_sends([(j, o, both) for j in v_items for o in (1, 0)]),
        "Vn": lambda: far_sends([(j, 0, both) for j in v_items]),
        "Va": lambda: far_sends([(j, 1, both) for j in v_items]),
    }

    def issue(names):
        for name in names:
            sends[name]()

    kinds = ("V", "K")
    for name in NEARS:
        mine_to_near(kinds.index(name)).start()
    for name in BESIDE:
        if name == "Q":
            q_sends(beside)
        else:
            own_sends(kinds.index(name), beside)
    by_place(lambda: issue(INNER_OWN + INNER_FAR), lambda: issue(OUTER))

    for h in range(heads):
        kv[ni, 0, h, me] = ks[mine, h]
    qg[place] = qs[mine]
    v_in.wait()

    scale = math.log2(math.e) / math.sqrt(dim)
    rows = groups * tokens

    def queries(h):
        own_text = [tqs[h, m] for m in range(PAIR)]
        return jnp.concatenate([qg[:, h].reshape(rows, dim)] + own_text, axis=0)

    def score(h, keys):
        return lax.dot_general(queries(h), keys, (((1,), (1,)), ((), ())), preferred_element_type=jnp.float32) * scale

    def block(w, n, f, h):
        return kv[n, w, h, pl.ds(f * groups, groups)].reshape(rows, dim)

    def weigh(f, h):
        sc = score(h, jnp.concatenate([block(0, ni, f, h), block(0, other, f, h)], axis=0))
        old = peak[h]
        top = jnp.maximum(old, jnp.max(sc, axis=1, keepdims=True))
        p = jnp.exp2(sc - top)
        factor = jnp.exp2(old - top)
        peak[h] = top
        total[h] = total[h] * factor + jnp.sum(p, axis=1, keepdims=True)
        acc[h] = acc[h] * factor
        return p.astype(jnp.bfloat16)

    def values(f, h):
        return jnp.concatenate([block(1, ni, f, h), block(1, other, f, h)], axis=0)

    def absorb(f, h):
        p = weigh(f, h)
        acc[h] += jnp.dot(p, values(f, h), preferred_element_type=jnp.float32)

    last = far - 1
    f_last = far_of(last)

    def from_inner(js, dhs):
        def go():
            for j in js:
                relay(last, j, 0, dhs)

        pl.when(jnp.logical_not(inner))(go)

    def whole(i):
        def fetch(order):
            for j in range(len(items)):
                for outward in order:
                    relay(i + 1, j, outward, both)

        def bulk():
            relay_bulk(i + 1, 1, both)
            relay_bulk(i + 1, 0, both)
            fetch((1,))

        by_place(bulk, lambda: fetch((0, 1)))
        for w in range(2):
            take_bulk(i + 1, w)
        for j in range(len(items)):
            take(i + 1, j)
        for h in range(heads):
            absorb(far_of(i + 1), h)

    def queries_in():
        with mark("qwait"):
            received(qg.at[pl.ds(0, groups - 1)], q_recv)
            for copy in text_in:
                copy.wait()
        with mark("text"):
            for h in range(heads):
                s = score(h, tks[h])
                live = lax.broadcasted_iota(jnp.int32, s.shape, 1) < count_ref[0]
                s = jnp.where(live, s, -jnp.inf)
                top = jnp.max(s, axis=1, keepdims=True)
                p = jnp.exp2(s - top)
                peak[h] = top
                total[h] = jnp.sum(p, axis=1, keepdims=True)
                acc[h] = jnp.dot(p.astype(jnp.bfloat16), tvs[h], preferred_element_type=jnp.float32)
        each(far - 2, whole)

    partner = lax.rem(mi + 1, PAIR)

    def finish(h):
        acc[h] += jnp.dot(probs[h, :, :rows], block(1, ni, f_last, h), preferred_element_type=jnp.float32)
        mixed = acc[h] + jnp.dot(probs[h, :, rows:], block(1, other, f_last, h), preferred_element_type=jnp.float32)
        result = (mixed / total[h]).astype(jnp.bfloat16)
        ost[h] = result[:rows].reshape(groups, tokens, dim)
        tst[h] = result[rows:].reshape(tst.shape[1:])
        for dm, dh in reversed(offsets):
            m, h2 = mate(dm, dh)
            remote(ost.at[h, m * hds + h2], out_ref.at[mine, h], o_send, o_recv, at(fi, m, ni, h2)).start()
        remote(tst.at[h, partner], tout_ref.at[mi, h], t_send, t_recv, at(fi, partner, ni, hd)).start()
        out_ref[mine, h] = ost[h, place]
        tout_ref[mi, h] = tst[h, mi]

    def own_step(j, which):
        def go():
            for dm, dh in which:
                own_relay(j, dm, dh)

        return go

    def at_inner(w, dhs):
        return lambda: pl.when(inner)(lambda: relay_bulk(last, w, dhs))

    def away(js):
        def go():
            for j in js:
                relay(last, j, 1, both)

        return go

    def per_head(lo, body):
        def go(h, _):
            body(h)
            return 0

        lax.fori_loop(lo, heads, go, 0)

    def own_weigh(h):
        held[h] = weigh(fi, h)

    def far_weigh(h):
        probs[h] = weigh(f_last, h)

    def own_mix(h):
        acc[h] += jnp.dot(held[h], values(fi, h), preferred_element_type=jnp.float32)

    def own_first():
        received(kv.at[other, 0, :, pl.ds(fi * groups, groups)], k_across)
        own_weigh(0)

    def own_values():
        received(kv.at[other, 1, :, pl.ds(fi * groups, groups)], v_across)
        per_head(0, own_mix)

    def far_first():
        take_bulk(last, 0)
        take(last, 0)
        far_weigh(0)

    def far_rest():
        for j in k_items[1:]:
            take(last, j)
        per_head(1, far_weigh)

    def finish_first():
        take_bulk(last, 1)
        take(last, v_items[0])
        finish(0)

    def finish_heads(hs):
        def go():
            for h in hs:
                take(last, v_items[h])
                finish(h)

        return go

    steps = {
        "vy": own_step(0, beside),
        "vz": own_step(0, ahead),
        "vd": own_step(0, askew),
        "ky": own_step(1, beside),
        "kz": own_step(1, ahead),
        "kd": own_step(1, askew),
        "bvz": at_inner(1, straight),
        "bvd": at_inner(1, skew),
        "bkz": at_inner(0, straight),
        "bkd": at_inner(0, skew),
        "nkz": lambda: from_inner(k_items, straight),
        "nkd": lambda: from_inner(k_items, skew),
        "nv0": lambda: from_inner(v_items[:1], both),
        "nv1": lambda: from_inner(v_items[1:2], both),
        "nv2": lambda: from_inner(v_items[2:], both),
        "fk0": away(k_items[:1]),
        "fk1": away(k_items[1:]),
        "fv0": away(v_items[:1]),
        "fv1": away(v_items[1:2]),
        "fv2": away(v_items[2:]),
        "q": queries_in,
        "ok0": own_first,
        "ok1": lambda: per_head(1, own_weigh),
        "ov": own_values,
        "w0": far_first,
        "w1": far_rest,
        "f0": finish_first,
        "f1": finish_heads(range(1, min(2, heads))),
        "f2": finish_heads(range(2, heads)),
    }
    for name in STEPS:
        with mark(name):
            steps[name]()

    with mark("sent"):
        left(kv.at[ni], own_send)
        left(kv.at[ni, :, :, pl.ds(0, far * groups - 1)], own_pass)
        left(qs.at[pl.ds(0, groups - 1)], q_send)
        left(ost.at[:, pl.ds(0, groups - 1)], o_send)
        left(tst.at[:, 0], t_send)
    with mark("outwait"):
        received(ost.at[:, pl.ds(0, groups - 1)], o_recv)
        received(tst.at[:, 0], t_recv)


def settle(out_ref, tout_ref, video_ref, text_ref, sems):
    blocks = out_ref.shape[0]
    copies = [pltpu.make_async_copy(out_ref.at[i], video_ref.at[i], sems.at[i]) for i in range(blocks)]
    copies.append(pltpu.make_async_copy(tout_ref, text_ref, sems.at[blocks]))
    for copy in copies:
        copy.start()
    for copy in copies:
        copy.wait()


def local(cores, ctxs, hds, video_q, video_k, video_v, positions, text_q, text_k, text_v, text_count):
    tokens, all_heads, dim = video_q.shape
    text = text_q.shape[0]
    groups = PAIR * hds
    heads = all_heads // groups
    far = ctxs // (PAIR * NEAR)
    share = text // ctxs
    rows = groups * tokens + PAIR * share
    freq, swap = constants(dim)

    def by_head(x):
        return jnp.swapaxes(x, 0, 1).reshape(groups, heads, tokens, dim)

    vmem = pl.BlockSpec(memory_space=pltpu.VMEM)
    dma = pltpu.SemaphoreType.DMA
    count = len(far_items(heads))
    out, tout = pl.pallas_call(
        functools.partial(kernel, cores, far, hds),
        name="joint_attention",
        out_shape=(
            pltpu.VMEM((groups, heads, tokens, dim), jnp.bfloat16),
            pltpu.VMEM((PAIR, heads, share, dim), jnp.bfloat16),
        ),
        in_specs=[pl.BlockSpec(memory_space=pl.ANY)] * 9 + [pl.BlockSpec(memory_space=pltpu.SMEM)],
        out_specs=(vmem, vmem),
        scratch_shapes=[
            pltpu.VMEM(positions.shape, jnp.int32),
            pltpu.VMEM((1, dim), jnp.float32),
            pltpu.VMEM((dim, dim), jnp.bfloat16),
            pltpu.VMEM((groups, heads, tokens, dim), jnp.bfloat16),
            pltpu.VMEM((groups, heads, tokens, dim), jnp.bfloat16),
            pltpu.VMEM((heads, PAIR, share, dim), jnp.bfloat16),
            pltpu.VMEM((heads, text, dim), jnp.bfloat16),
            pltpu.VMEM((heads, text, dim), jnp.bfloat16),
            pltpu.VMEM((groups, heads, tokens, dim), jnp.bfloat16),
            pltpu.VMEM((groups, heads, tokens, dim), jnp.bfloat16),
            pltpu.VMEM((groups, heads, tokens, dim), jnp.bfloat16),
            pltpu.VMEM((NEAR, 2, heads, far * groups, tokens, dim), jnp.bfloat16),
            pltpu.VMEM((heads, groups, tokens, dim), jnp.bfloat16),
            pltpu.VMEM((heads, PAIR, share, dim), jnp.bfloat16),
            pltpu.VMEM((heads, rows, dim), jnp.float32),
            pltpu.VMEM((heads, rows, 1), jnp.float32),
            pltpu.VMEM((heads, rows, 1), jnp.float32),
            pltpu.VMEM((heads, rows, 2 * groups * tokens), jnp.bfloat16),
            pltpu.VMEM((heads, rows, 2 * groups * tokens), jnp.bfloat16),
            dma((8 + PAIR,)),
            dma((2, PAIR, hds)),
            dma((count, far - 1, PAIR, hds)),
            dma((count, far - 1)),
            dma((2, far - 1, hds)),
            dma((2, far - 1)),
            dma((10,)),
        ],
        compiler_params=pltpu.CompilerParams(
            collective_id=0, has_side_effects=True, vmem_limit_bytes=60 * 1024 * 1024
        ),
    )(
        by_head(video_q), by_head(video_k), by_head(video_v),
        jnp.swapaxes(text_q, 0, 1).reshape(PAIR * heads, ctxs, share, dim), jnp.swapaxes(text_k, 0, 1), jnp.swapaxes(text_v, 0, 1),
        positions, jnp.asarray(freq[None, :]), jnp.asarray(swap, jnp.bfloat16), text_count,
    )
    out, tout = pl.pallas_call(
        settle,
        name="settle",
        out_shape=(jax.ShapeDtypeStruct(out.shape, out.dtype), jax.ShapeDtypeStruct(tout.shape, tout.dtype)),
        in_specs=[vmem] * 2,
        out_specs=(pl.BlockSpec(memory_space=pl.ANY),) * 2,
        scratch_shapes=[dma((groups + 1,))],
    )(pltpu.with_memory_space_constraint(out, pltpu.VMEM), pltpu.with_memory_space_constraint(tout, pltpu.VMEM))
    video_out = jnp.swapaxes(out.reshape(all_heads, tokens, dim), 0, 1)
    text_out = jnp.swapaxes(tout.reshape(PAIR * heads, share, dim), 0, 1)
    return (video_out, text_out)


def solution(mesh):
    return jax.shard_map(
        functools.partial(local, mesh.shape["grp"], mesh.shape["ctx"], mesh.shape["hd"]),
        mesh=mesh,
        in_specs=(
            P(("ctx", "hd"), "grp", None),
            P(("ctx", "hd"), "grp", None),
            P(("ctx", "hd"), "grp", None),
            P(None, ("ctx", "hd")),
            P(None, ("grp", "hd"), None),
            P(None, ("grp", "hd"), None),
            P(None, ("grp", "hd"), None),
            P(),
        ),
        out_specs=(P(("ctx", "hd"), "grp", None), P("ctx", ("grp", "hd"), None)),
        check_vma=False,
    )
```

```python
import contextlib
import functools
import math

import jax
import jax.numpy as jnp
import numpy as np
from jax import lax
from jax.experimental import pallas as pl
from jax.experimental.pallas import tpu as pltpu
from jax.sharding import PartitionSpec as P

THETA = 256.0
MESH = pl.DeviceIdType.MESH
NEARS = ('V', 'K')
BESIDE = ('Q', 'V', 'K')
INNER_OWN = ('Vz', 'Qz', 'Kz', 'Vd', 'Kd', 'Qd')
INNER_FAR = ('bVz', 'bKz', 'aKz', 'bVd', 'bKd', 'aKd', 'aV')
OUTER = ('Vz', 'Kz', 'Qz', 'Vd', 'Qd', 'Kd', 'Kn', 'Ka', 'V')
STEPS = ('vz', 'vy', 'ky', 'bvz', 'kz', 'bkz', 'nkz', 'vd', 'bvd', 'kd', 'bkd', 'q', 'nkd', 'fk0', 'ok0', 'fk1', 'fv0', 'ok1', 'ov', 'fv1', 'w0', 'fv2', 'nv0', 'nv1', 'nv2', 'w1', 'f0', 'f1', 'f2')
PAIR = 2
NEAR = 2


def bands(dim):
    band_t = dim // 8
    band_h = (dim - band_t) // 2
    return (band_t, band_h, dim - band_t - band_h)


def constants(dim):
    freq = np.zeros((dim,), np.float32)
    swap = np.zeros((dim, dim), np.float32)
    start = 0
    for size in bands(dim):
        half = size // 2
        for i in range(half):
            low, high = start + i, start + half + i
            freq[low] = freq[high] = np.float32(THETA ** (-2.0 * i / size))
            swap[high, low] = -1.0
            swap[low, high] = 1.0
        start += size
    return freq, swap


def each(count, body):
    if count <= 4:
        for i in range(count):
            body(i)
    else:
        lax.fori_loop(0, count, lambda i, _: (body(i), 0)[1], 0)


def mark(name):
    return contextlib.nullcontext()


def far_items(heads):
    return [(0, 0, heads)] + [(1, h, h + 1) for h in range(heads)]


def kernel(cores, far, hds, q_ref, k_ref, v_ref, tq_ref, tk_ref, tv_ref, pos_in, freq_in, swap_in, count_ref,
           out_ref, tout_ref, pos_ref, freq_ref, swap_ref, qin, kin, tqs, tks, tvs, qs, ks, qg, kv, ost, tst, acc, peak, total, held, probs,
           in_sems, own_recv, far_recv, far_across, bulk_recv, bulk_across, once):
    ctx = lax.axis_index("ctx")
    hd = lax.axis_index("hd")
    fi, mi, ni = ctx // (PAIR * NEAR), (ctx // NEAR) % PAIR, ctx % NEAR
    groups = PAIR * hds
    heads = v_ref.shape[1]
    tokens, dim = v_ref.shape[2], v_ref.shape[3]
    other = lax.rem(ni + 1, NEAR)
    mine = hd * PAIR + mi
    place = mi * hds + hd
    own_items = [(1, 0, heads), (0, 0, heads)]
    items = far_items(heads)
    inner = lax.rem(fi + mi, 2) == 1
    q_send, q_recv, own_send, own_pass, v_across, k_across, o_send, o_recv, t_send, t_recv = (
        once.at[i] for i in range(10))
    own_across = (v_across, k_across)

    def at(f, m, n, h):
        return {"ctx": (f * PAIR + m) * NEAR + n, "hd": h}

    near = at(fi, mi, other, hd)
    offsets = [(0, dh) for dh in range(1, hds)] + [(dm, dh) for dm in range(1, PAIR) for dh in range(hds)]

    def mate(dm, dh):
        return lax.rem(mi + dm, PAIR), lax.rem(hd + dh, hds)

    def far_of(i):
        return lax.rem(fi + i, far)

    def side(f, outward):
        return lax.rem(f + 1 + outward, PAIR)

    text_heads = pl.ds(mi * heads, heads)
    k_in = pltpu.make_async_copy(k_ref, kin, in_sems.at[0])
    q_in = pltpu.make_async_copy(q_ref, qin, in_sems.at[1])
    v_in = pltpu.make_async_copy(v_ref.at[mine], kv.at[ni, 1, :, fi * groups + place], in_sems.at[2])
    text_in = tuple(
        pltpu.make_async_copy(tq_ref.at[text_heads, (fi * PAIR + m) * NEAR + ni], tqs.at[:, m], in_sems.at[8 + m])
        for m in range(PAIR)
    ) + (
        pltpu.make_async_copy(tk_ref.at[text_heads], tks, in_sems.at[3]),
        pltpu.make_async_copy(tv_ref.at[text_heads], tvs, in_sems.at[4]),
    )
    table_in = (
        pltpu.make_async_copy(pos_in, pos_ref, in_sems.at[5]),
        pltpu.make_async_copy(freq_in, freq_ref, in_sems.at[6]),
        pltpu.make_async_copy(swap_in, swap_ref, in_sems.at[7]),
    )
    barrier = pltpu.get_barrier_semaphore()

    def greet(peer):
        for g in range(cores):
            pl.semaphore_signal(barrier, inc=1, device_id=dict(peer, grp=g), device_id_type=MESH)

    def greet_far(i):
        for m in range(PAIR):
            for h in range(hds):
                greet(at(far_of(i + 1), m, ni, h))

    each(far - 1, greet_far)
    for dm, dh in offsets:
        m, h = mate(dm, dh)
        greet(at(fi, m, ni, h))
    greet(near)
    for copy in table_in + (k_in, q_in, v_in) + text_in:
        copy.start()
    with mark("tablewait"):
        for copy in table_in:
            copy.wait()
    swap = swap_ref[...]
    diagonal = (lax.broadcasted_iota(jnp.int32, (tokens, tokens), 0)
                == lax.broadcasted_iota(jnp.int32, (tokens, tokens), 1))
    lane = lax.broadcasted_iota(jnp.int32, (tokens, dim), 1)

    def column(axis):
        row = pos_ref[axis:axis + 1, :].astype(jnp.float32)
        return jnp.sum(jnp.where(diagonal, row, 0.0), axis=1, keepdims=True)

    band_t, band_h, _ = bands(dim)
    angle = jnp.where(lane < band_t, column(0), jnp.where(lane < band_t + band_h, column(1), column(2))) * freq_ref[...]
    cos, sin = jnp.cos(angle), jnp.sin(angle)

    def rotate(src, dst):
        for g in range(groups):
            for h in range(heads):
                x = src[g, h]
                turned = jnp.dot(x, swap, preferred_element_type=jnp.float32)
                dst[g, h] = (x.astype(jnp.float32) * cos + turned * sin).astype(jnp.bfloat16)

    with mark("rot"):
        k_in.wait()
        rotate(kin, ks)
        q_in.wait()
        rotate(qin, qs)
    with mark("barrier"):
        pl.semaphore_wait(barrier, cores * ((groups - 1) + (far - 1) * groups + 1))

    def remote(src, dst, send, recv, peer):
        return pltpu.make_async_remote_copy(src_ref=src, dst_ref=dst, send_sem=send, recv_sem=recv,
                                            device_id=peer, device_id_type=MESH)

    def received(ref, sem):
        remote(ref, ref, own_send, sem, near).wait_recv()

    def left(ref, sem):
        remote(ref, ref, sem, v_across, near).wait_send()

    def source(w, g, lo, hi):
        return (ks if w == 0 else v_ref).at[g, pl.ds(lo, hi - lo)]

    def part(n, w, lo, hi, s, count=None):
        return kv.at[n, w, pl.ds(lo, hi - lo), s if count is None else pl.ds(s, count)]

    me = fi * groups + place

    def own_to_mate(j, dm, dh):
        w, lo, hi = own_items[j]
        m, h = mate(dm, dh)
        return remote(source(w, h * PAIR + m, lo, hi), part(ni, w, lo, hi, me), own_send, own_recv.at[j, dm, dh], at(fi, m, ni, h))

    def mine_to_near(j):
        w, lo, hi = own_items[j]
        return remote(source(w, mine, lo, hi), part(ni, w, lo, hi, me), own_send, own_across[j], near)

    def pass_on(block, arrive, send, across):
        received(block, arrive)
        remote(block, block, send, across, near).start()

    def own_relay(j, dm, dh):
        w, lo, hi = own_items[j]
        m, h = lax.rem(mi + PAIR - dm, PAIR), lax.rem(hd + hds - dh, hds)
        pass_on(part(ni, w, lo, hi, fi * groups + m * hds + h), own_recv.at[j, dm, dh], own_pass, own_across[j])

    def far_send_one(j, i, outward, dhs):
        w, lo, hi = items[j] if j >= 0 else (j + 2, 0, heads)
        f = far_of(i)
        m = side(f, outward)
        for dh in dhs:
            h = lax.rem(hd + dh, hds)
            arrive = far_recv.at[j, far - i - 1, mi, dh] if j >= 0 else bulk_recv.at[j + 2, far - i - 1, dh]
            remote(source(w, h * PAIR + m, lo, hi), part(ni, w, lo, hi, me), own_send, arrive,
                   at(f, m, ni, h)).start()

    def far_sends(order):
        def send(i):
            for j, outward, dhs in order:
                far_send_one(j, i + 1, outward, dhs)

        each(far - 1, send)

    def relay(i, j, outward, dhs):
        w, lo, hi = items[j]
        f = far_of(i)
        m = side(f, outward)
        for dh in dhs:
            pass_on(part(ni, w, lo, hi, f * groups + m * hds + lax.rem(hd + hds - dh, hds)), far_recv.at[j, i - 1, m, dh],
                    own_pass, far_across.at[j, i - 1])

    def take(i, j):
        w, lo, hi = items[j]

        @pl.when(inner)
        def _():
            received(part(other, w, lo, hi, far_of(i) * groups, hds), far_across.at[j, i - 1])

        @pl.when(jnp.logical_not(inner))
        def _():
            received(part(other, w, lo, hi, far_of(i) * groups, groups), far_across.at[j, i - 1])

    def relay_bulk(i, w, dhs):
        f = far_of(i)
        for dh in dhs:
            pass_on(part(ni, w, 0, heads, f * groups + side(f, 0) * hds + lax.rem(hd + hds - dh, hds)),
                    bulk_recv.at[w, i - 1, dh], own_pass, bulk_across.at[w, i - 1])

    def take_bulk(i, w):
        @pl.when(inner)
        def _():
            received(part(other, w, 0, heads, far_of(i) * groups, hds), bulk_across.at[w, i - 1])

    def by_place(near_side, far_side):
        @pl.when(inner)
        def _():
            near_side()

        @pl.when(jnp.logical_not(inner))
        def _():
            far_side()

    def q_to_mate(dm, dh):
        m, h = mate(dm, dh)
        return remote(qs.at[h * PAIR + m], qg.at[place], q_send, q_recv, at(fi, m, ni, h))

    beside = [(0, dh) for dh in range(1, hds)]
    ahead = [(dm, 0) for dm in range(1, PAIR)]
    askew = [(dm, dh) for dm in range(1, PAIR) for dh in range(1, hds)]
    straight, skew, both = (0,), tuple(range(1, hds)), tuple(range(hds))

    def own_sends(j, which):
        for dm, dh in which:
            own_to_mate(j, dm, dh).start()

    def q_sends(which):
        for dm, dh in which:
            q_to_mate(dm, dh).start()


    k_items = [j for j, item in enumerate(items) if item[0] == 0]
    v_items = [j for j, item in enumerate(items) if item[0] == 1]
    sends = {
        "Vz": lambda: own_sends(0, ahead),
        "Kz": lambda: own_sends(1, ahead),
        "Kd": lambda: own_sends(1, askew),
        "Vd": lambda: own_sends(0, askew),
        "Qz": lambda: q_sends(ahead),
        "Qd": lambda: q_sends(askew),
        "bVz": lambda: far_sends([(-1, 0, straight)]),
        "bKz": lambda: far_sends([(-2, 0, straight)]),
        "bKd": lambda: far_sends([(-2, 0, skew)]),
        "bVd": lambda: far_sends([(-1, 0, skew)]),
        "aKz": lambda: far_sends([(j, 1, straight) for j in k_items]),
        "aKd": lambda: far_sends([(j, 1, skew) for j in k_items]),
        "aV": lambda: far_sends([(j, 1, both) for j in v_items]),
        "aV0": lambda: far_sends([(j, 1, both) for j in v_items[:1]]),
        "aV1": lambda: far_sends([(j, 1, both) for j in v_items[1:]]),
        "V0": lambda: far_sends([(j, o, both) for j in v_items[:1] for o in (0, 1)]),
        "V1": lambda: far_sends([(j, o, both) for j in v_items[1:] for o in (0, 1)]),
        "aVz": lambda: far_sends([(j, 1, straight) for j in v_items]),
        "aVd": lambda: far_sends([(j, 1, skew) for j in v_items]),
        "K": lambda: far_sends([(j, o, both) for j in k_items for o in (0, 1)]),
        "Kn": lambda: far_sends([(j, 0, both) for j in k_items]),
        "Ka": lambda: far_sends([(j, 1, both) for j in k_items]),
        "V": lambda: far_sends([(j, o, both) for j in v_items for o in (0, 1)]),
        "W": lambda: far_sends([(j, o, both) for j in v_items for o in (1, 0)]),
        "Vn": lambda: far_sends([(j, 0, both) for j in v_items]),
        "Va": lambda: far_sends([(j, 1, both) for j in v_items]),
    }

    def issue(names):
        for name in names:
            sends[name]()

    kinds = ("V", "K")
    for name in NEARS:
        mine_to_near(kinds.index(name)).start()
    for name in BESIDE:
        if name == "Q":
            q_sends(beside)
        else:
            own_sends(kinds.index(name), beside)
    by_place(lambda: issue(INNER_OWN + INNER_FAR), lambda: issue(OUTER))

    for h in range(heads):
        kv[ni, 0, h, me] = ks[mine, h]
    qg[place] = qs[mine]
    v_in.wait()

    scale = math.log2(math.e) / math.sqrt(dim)
    rows = groups * tokens

    def queries(h):
        own_text = [tqs[h, m] for m in range(PAIR)]
        return jnp.concatenate([qg[:, h].reshape(rows, dim)] + own_text, axis=0)

    def score(h, keys):
        return lax.dot_general(queries(h), keys, (((1,), (1,)), ((), ())), preferred_element_type=jnp.float32) * scale

    def block(w, n, f, h):
        return kv[n, w, h, pl.ds(f * groups, groups)].reshape(rows, dim)

    def weigh(f, h):
        sc = score(h, jnp.concatenate([block(0, ni, f, h), block(0, other, f, h)], axis=0))
        old = peak[h]
        top = jnp.maximum(old, jnp.max(sc, axis=1, keepdims=True))
        p = jnp.exp2(sc - top)
        factor = jnp.exp2(old - top)
        peak[h] = top
        total[h] = total[h] * factor + jnp.sum(p, axis=1, keepdims=True)
        acc[h] = acc[h] * factor
        return p.astype(jnp.bfloat16)

    def values(f, h):
        return jnp.concatenate([block(1, ni, f, h), block(1, other, f, h)], axis=0)

    def absorb(f, h):
        p = weigh(f, h)
        acc[h] += jnp.dot(p, values(f, h), preferred_element_type=jnp.float32)

    last = far - 1
    f_last = far_of(last)

    def from_inner(js, dhs):
        def go():
            for j in js:
                relay(last, j, 0, dhs)

        pl.when(jnp.logical_not(inner))(go)

    def whole(i):
        def fetch(order):
            for j in range(len(items)):
                for outward in order:
                    relay(i + 1, j, outward, both)

        def bulk():
            relay_bulk(i + 1, 1, both)
            relay_bulk(i + 1, 0, both)
            fetch((1,))

        by_place(bulk, lambda: fetch((0, 1)))
        for w in range(2):
            take_bulk(i + 1, w)
        for j in range(len(items)):
            take(i + 1, j)
        for h in range(heads):
            absorb(far_of(i + 1), h)

    def queries_in():
        with mark("qwait"):
            received(qg.at[pl.ds(0, groups - 1)], q_recv)
            for copy in text_in:
                copy.wait()
        with mark("text"):
            for h in range(heads):
                s = score(h, tks[h])
                live = lax.broadcasted_iota(jnp.int32, s.shape, 1) < count_ref[0]
                s = jnp.where(live, s, -jnp.inf)
                top = jnp.max(s, axis=1, keepdims=True)
                p = jnp.exp2(s - top)
                peak[h] = top
                total[h] = jnp.sum(p, axis=1, keepdims=True)
                acc[h] = jnp.dot(p.astype(jnp.bfloat16), tvs[h], preferred_element_type=jnp.float32)
        each(far - 2, whole)

    partner = lax.rem(mi + 1, PAIR)

    def finish(h):
        acc[h] += jnp.dot(probs[h, :, :rows], block(1, ni, f_last, h), preferred_element_type=jnp.float32)
        mixed = acc[h] + jnp.dot(probs[h, :, rows:], block(1, other, f_last, h), preferred_element_type=jnp.float32)
        result = (mixed / total[h]).astype(jnp.bfloat16)
        ost[h] = result[:rows].reshape(groups, tokens, dim)
        tst[h] = result[rows:].reshape(tst.shape[1:])
        for dm, dh in reversed(offsets):
            m, h2 = mate(dm, dh)
            remote(ost.at[h, m * hds + h2], out_ref.at[mine, h], o_send, o_recv, at(fi, m, ni, h2)).start()
        remote(tst.at[h, partner], tout_ref.at[mi, h], t_send, t_recv, at(fi, partner, ni, hd)).start()
        out_ref[mine, h] = ost[h, place]
        tout_ref[mi, h] = tst[h, mi]

    def own_step(j, which):
        def go():
            for dm, dh in which:
                own_relay(j, dm, dh)

        return go

    def at_inner(w, dhs):
        return lambda: pl.when(inner)(lambda: relay_bulk(last, w, dhs))

    def away(js):
        def go():
            for j in js:
                relay(last, j, 1, both)

        return go

    def per_head(lo, body):
        def go(h, _):
            body(h)
            return 0

        lax.fori_loop(lo, heads, go, 0)

    def own_weigh(h):
        held[h] = weigh(fi, h)

    def far_weigh(h):
        probs[h] = weigh(f_last, h)

    def own_mix(h):
        acc[h] += jnp.dot(held[h], values(fi, h), preferred_element_type=jnp.float32)

    def own_first():
        received(kv.at[other, 0, :, pl.ds(fi * groups, groups)], k_across)
        own_weigh(0)

    def own_values():
        received(kv.at[other, 1, :, pl.ds(fi * groups, groups)], v_across)
        per_head(0, own_mix)

    def far_first():
        take_bulk(last, 0)
        take(last, 0)
        far_weigh(0)

    def far_rest():
        for j in k_items[1:]:
            take(last, j)
        per_head(1, far_weigh)

    def finish_first():
        take_bulk(last, 1)
        take(last, v_items[0])
        finish(0)

    def finish_heads(hs):
        def go():
            for h in hs:
                take(last, v_items[h])
                finish(h)

        return go

    steps = {
        "vy": own_step(0, beside),
        "vz": own_step(0, ahead),
        "vd": own_step(0, askew),
        "ky": own_step(1, beside),
        "kz": own_step(1, ahead),
        "kd": own_step(1, askew),
        "bvz": at_inner(1, straight),
        "bvd": at_inner(1, skew),
        "bkz": at_inner(0, straight),
        "bkd": at_inner(0, skew),
        "nkz": lambda: from_inner(k_items, straight),
        "nkd": lambda: from_inner(k_items, skew),
        "nv0": lambda: from_inner(v_items[:1], both),
        "nv1": lambda: from_inner(v_items[1:2], both),
        "nv2": lambda: from_inner(v_items[2:], both),
        "fk0": away(k_items[:1]),
        "fk1": away(k_items[1:]),
        "fv0": away(v_items[:1]),
        "fv1": away(v_items[1:2]),
        "fv2": away(v_items[2:]),
        "q": queries_in,
        "ok0": own_first,
        "ok1": lambda: per_head(1, own_weigh),
        "ov": own_values,
        "w0": far_first,
        "w1": far_rest,
        "f0": finish_first,
        "f1": finish_heads(range(1, min(2, heads))),
        "f2": finish_heads(range(2, heads)),
    }
    for name in STEPS:
        with mark(name):
            steps[name]()

    with mark("sent"):
        left(kv.at[ni], own_send)
        left(kv.at[ni, :, :, pl.ds(0, far * groups - 1)], own_pass)
        left(qs.at[pl.ds(0, groups - 1)], q_send)
        left(ost.at[:, pl.ds(0, groups - 1)], o_send)
        left(tst.at[:, 0], t_send)
    with mark("outwait"):
        received(ost.at[:, pl.ds(0, groups - 1)], o_recv)
        received(tst.at[:, 0], t_recv)


def settle(out_ref, tout_ref, video_ref, text_ref, sems):
    blocks = out_ref.shape[0]
    copies = [pltpu.make_async_copy(out_ref.at[i], video_ref.at[i], sems.at[i]) for i in range(blocks)]
    copies.append(pltpu.make_async_copy(tout_ref, text_ref, sems.at[blocks]))
    for copy in copies:
        copy.start()
    for copy in copies:
        copy.wait()


def local(cores, ctxs, hds, video_q, video_k, video_v, positions, text_q, text_k, text_v, text_count):
    tokens, all_heads, dim = video_q.shape
    text = text_q.shape[0]
    groups = PAIR * hds
    heads = all_heads // groups
    far = ctxs // (PAIR * NEAR)
    share = text // ctxs
    rows = groups * tokens + PAIR * share
    freq, swap = constants(dim)

    def by_head(x):
        return jnp.swapaxes(x, 0, 1).reshape(groups, heads, tokens, dim)

    vmem = pl.BlockSpec(memory_space=pltpu.VMEM)
    dma = pltpu.SemaphoreType.DMA
    count = len(far_items(heads))
    out, tout = pl.pallas_call(
        functools.partial(kernel, cores, far, hds),
        name="joint_attention",
        out_shape=(
            pltpu.VMEM((groups, heads, tokens, dim), jnp.bfloat16),
            pltpu.VMEM((PAIR, heads, share, dim), jnp.bfloat16),
        ),
        in_specs=[pl.BlockSpec(memory_space=pl.ANY)] * 9 + [pl.BlockSpec(memory_space=pltpu.SMEM)],
        out_specs=(vmem, vmem),
        scratch_shapes=[
            pltpu.VMEM(positions.shape, jnp.int32),
            pltpu.VMEM((1, dim), jnp.float32),
            pltpu.VMEM((dim, dim), jnp.bfloat16),
            pltpu.VMEM((groups, heads, tokens, dim), jnp.bfloat16),
            pltpu.VMEM((groups, heads, tokens, dim), jnp.bfloat16),
            pltpu.VMEM((heads, PAIR, share, dim), jnp.bfloat16),
            pltpu.VMEM((heads, text, dim), jnp.bfloat16),
            pltpu.VMEM((heads, text, dim), jnp.bfloat16),
            pltpu.VMEM((groups, heads, tokens, dim), jnp.bfloat16),
            pltpu.VMEM((groups, heads, tokens, dim), jnp.bfloat16),
            pltpu.VMEM((groups, heads, tokens, dim), jnp.bfloat16),
            pltpu.VMEM((NEAR, 2, heads, far * groups, tokens, dim), jnp.bfloat16),
            pltpu.VMEM((heads, groups, tokens, dim), jnp.bfloat16),
            pltpu.VMEM((heads, PAIR, share, dim), jnp.bfloat16),
            pltpu.VMEM((heads, rows, dim), jnp.float32),
            pltpu.VMEM((heads, rows, 1), jnp.float32),
            pltpu.VMEM((heads, rows, 1), jnp.float32),
            pltpu.VMEM((heads, rows, 2 * groups * tokens), jnp.bfloat16),
            pltpu.VMEM((heads, rows, 2 * groups * tokens), jnp.bfloat16),
            dma((8 + PAIR,)),
            dma((2, PAIR, hds)),
            dma((count, far - 1, PAIR, hds)),
            dma((count, far - 1)),
            dma((2, far - 1, hds)),
            dma((2, far - 1)),
            dma((10,)),
        ],
        compiler_params=pltpu.CompilerParams(
            collective_id=0, has_side_effects=True, vmem_limit_bytes=60 * 1024 * 1024
        ),
    )(
        by_head(video_q), by_head(video_k), by_head(video_v),
        jnp.swapaxes(text_q, 0, 1).reshape(PAIR * heads, ctxs, share, dim), jnp.swapaxes(text_k, 0, 1), jnp.swapaxes(text_v, 0, 1),
        positions, jnp.asarray(freq[None, :]), jnp.asarray(swap, jnp.bfloat16), text_count,
    )
    out, tout = pl.pallas_call(
        settle,
        name="settle",
        out_shape=(jax.ShapeDtypeStruct(out.shape, out.dtype), jax.ShapeDtypeStruct(tout.shape, tout.dtype)),
        in_specs=[vmem] * 2,
        out_specs=(pl.BlockSpec(memory_space=pl.ANY),) * 2,
        scratch_shapes=[dma((groups + 1,))],
    )(pltpu.with_memory_space_constraint(out, pltpu.VMEM), pltpu.with_memory_space_constraint(tout, pltpu.VMEM))
    video_out = jnp.swapaxes(out.reshape(all_heads, tokens, dim), 0, 1)
    text_out = jnp.swapaxes(tout.reshape(PAIR * heads, share, dim), 0, 1)
    return (video_out, text_out)


def solution(mesh):
    return jax.shard_map(
        functools.partial(local, mesh.shape["grp"], mesh.shape["ctx"], mesh.shape["hd"]),
        mesh=mesh,
        in_specs=(
            P(("ctx", "hd"), "grp", None),
            P(("ctx", "hd"), "grp", None),
            P(("ctx", "hd"), "grp", None),
            P(None, ("ctx", "hd")),
            P(None, ("grp", "hd"), None),
            P(None, ("grp", "hd"), None),
            P(None, ("grp", "hd"), None),
            P(),
        ),
        out_specs=(P(("ctx", "hd"), "grp", None), P("ctx", ("grp", "hd"), None)),
        check_vma=False,
    )
```
